512 devices in a mesh: dp: 4 (over x), gx: 8 (over y), gy: 16 (over z, core).
Axes of the slice: x: 4, y: 8, z: 8, core: 2. Of those that a mesh axis runs over, the one named last changes fastest.
Arguments:
- fields: float32 [4, 20, 32, 32, 512], P('dp', None, 'gx', 'gy'), may hold values from -6 to 6
- cotangent: float32 [4, 20, 32, 32, 512], P('dp', None, 'gx', 'gy'), may hold values from -6 to 6
- spectral: float32 [2, 72, 16, 12, 20, 20], P(None, 'gx', 'gy'), may hold values from -6 to 6
- bypass: float32 [20, 20], replicated, may hold values from -1.25 to 1.25
Outputs:
- outputs: float32 [4, 20, 32, 32, 512], P('dp', None, 'gx', 'gy')
- field_grad: float32 [4, 20, 32, 32, 512], P('dp', None, 'gx', 'gy')
- spectral_grad: float32 [2, 72, 16, 12, 20, 20], P(None, 'gx', 'gy')
The draws below stay inside these ranges and needn't reach their ends.
All inputs are finite; a program needn't handle non-finite values.
Results may differ from the reference program's by a relative error of at most 0.00011.
Values sent between devices are 32-bit elements; how exact they have to be, the bound alone decides.
No kernel may reach another device: no remote copies, remote signals or barrier semaphores. Data moves between devices by JAX's collectives and lax.ppermute only.
A program may use at most 64 MiB of HBM per device.

```python
import math
import jax
import jax.numpy as jnp
from jax import lax

WIDTH = 20
DEPTH = 64
STEPS = 8
MODES_X = 12
MODES_Y = 12
MODES_Z = 12
MODES_T = 8
NXG = 32
NYG = 32
ZT = 512
MZT = 96
MZT_PART = 6
QY = 72
BATCH = 4
N_GY = 16


def levels(stream_key, shape, cuts, smallest, high):
    level, own = 1.0, jax.random.fold_in(stream_key, 6)
    for position, shards_of in cuts:
        steps = jnp.exp(jax.random.uniform(jax.random.fold_in(own, position), (shards_of,), jnp.float32, smallest / len(cuts), high / len(cuts)))
        level = level * jnp.repeat(steps, shape[position] // shards_of).reshape([-1 if axis == position else 1 for axis in range(len(shape))])
    return level


def gaussian(own_key, extent, scale, most, pieces=(), kind=jnp.bfloat16):
    values = scale * jax.random.normal(own_key, extent, jnp.float32)
    if pieces:
        values = values * levels(own_key, extent, pieces, -0.22, 0.18)
    return jnp.clip(values, -most, most).astype(kind)


def setup_inputs(seed: int = 0) -> dict:
    keys = jax.random.split(jax.random.key(seed), 5)
    return {
        "fields": gaussian(keys[0], (BATCH, WIDTH, NXG, NYG, ZT), 1.0, 6.0, ((0, 4), (2, 8), (3, 16)), jnp.float32),
        "cotangent": gaussian(keys[1], (BATCH, WIDTH, NXG, NYG, ZT), 1.0, 6.0, ((0, 4), (2, 8), (3, 16)), jnp.float32),
        "spectral": gaussian(keys[2], (2, QY, N_GY, MODES_X, WIDTH, WIDTH), 1.0, 6.0, ((1, 8), (2, 16)), jnp.float32),
        "bypass": gaussian(keys[3], (WIDTH, WIDTH), WIDTH ** -0.5, 1.25, (), jnp.float32),
    }


exact_mode = lax.Precision.HIGHEST

def frequencies(amount):
    indices = jnp.arange(amount, dtype=jnp.int32)
    return jnp.where(indices < amount // 2, indices, indices - amount)

def phases(freqs, positions, length):
    windings = freqs[:, None] * positions[None, :] % length
    angles = windings.astype(jnp.float32) * (2.0 * math.pi / length)
    return (jnp.cos(angles), jnp.sin(angles))

def depth_table(depth_cells, step_cells, modes_depth, modes_time):
    cell_ids = jnp.arange(depth_cells * step_cells, dtype=jnp.int32)
    mode_ids = jnp.arange(modes_depth * modes_time, dtype=jnp.int32)
    first = mode_ids // modes_time
    second = mode_ids % modes_time
    freq_z = jnp.where(first < modes_depth // 2, first, first - modes_depth)
    freq_t = jnp.where(second < modes_time // 2, second, second - modes_time)
    depth_pos = cell_ids // step_cells
    time_pos = cell_ids % step_cells
    windings = (freq_z[None, :] * depth_pos[:, None] * step_cells + freq_t[None, :] * time_pos[:, None] * depth_cells) % (depth_cells * step_cells)
    angles = windings.astype(jnp.float32) * (2.0 * math.pi / (depth_cells * step_cells))
    return (jnp.cos(angles), jnp.sin(angles))

def rotate_sum(pattern, cosine, sines, real_part, imag_part, sign):
    cos_real = jnp.einsum(pattern, cosine, real_part, precision=exact_mode)
    cos_imag = jnp.einsum(pattern, cosine, imag_part, precision=exact_mode)
    sin_real = jnp.einsum(pattern, sines, real_part, precision=exact_mode)
    sin_imag = jnp.einsum(pattern, sines, imag_part, precision=exact_mode)
    return (cos_real - sign * sin_imag, cos_imag + sign * sin_real)

def reference(fields, cotangent, spectral, bypass):
    cos_zt, sin_zt = depth_table(DEPTH, STEPS, MODES_Z, MODES_T)
    cos_y, sin_y = phases(frequencies(MODES_Y), jnp.arange(NYG, dtype=jnp.int32), NYG)
    cos_x, sin_x = phases(frequencies(MODES_X), jnp.arange(NXG, dtype=jnp.int32), NXG)
    cell_count = NXG * NYG * ZT

    def fourier_layer(sample, weights):
        depth_real = jnp.einsum('cxyr,rm->cxym', sample, cos_zt, precision=exact_mode)
        depth_imag = -jnp.einsum('cxyr,rm->cxym', sample, sin_zt, precision=exact_mode)
        along_real, along_imag = rotate_sum('ly,cxym->cxlm', cos_y, sin_y, depth_real, depth_imag, -1.0)
        spec_real, spec_imag = rotate_sum('kx,cxlm->clkm', cos_x, sin_x, along_real, along_imag, -1.0)
        weight_real = weights[0]
        weight_imag = weights[1]
        mixing = 'clkm,lkmco->olkm'
        mixed_real = jnp.einsum(mixing, spec_real, weight_real, precision=exact_mode) - jnp.einsum(mixing, spec_imag, weight_imag, precision=exact_mode)
        mixed_imag = jnp.einsum(mixing, spec_real, weight_imag, precision=exact_mode) + jnp.einsum(mixing, spec_imag, weight_real, precision=exact_mode)
        back_real, back_imag = rotate_sum('kx,olkm->olxm', cos_x, sin_x, mixed_real, mixed_imag, 1.0)
        cell_real, cell_imag = rotate_sum('ly,olxm->oxym', cos_y, sin_y, back_real, back_imag, 1.0)
        spectral_part = (jnp.einsum('oxym,rm->oxyr', cell_real, cos_zt, precision=exact_mode) - jnp.einsum('oxym,rm->oxyr', cell_imag, sin_zt, precision=exact_mode)) / cell_count
        pre = spectral_part + jnp.einsum('cxyr,co->oxyr', sample, bypass, precision=exact_mode)
        return jax.nn.gelu(pre)

    def objective(field_all, weight_all):
        shaped = weight_all.reshape(2, MODES_Y, MZT_PART, N_GY, MODES_X, WIDTH, WIDTH)
        shaped = jnp.transpose(shaped, (0, 1, 4, 3, 2, 5, 6)).reshape(2, MODES_Y, MODES_X, MZT, WIDTH, WIDTH)
        return lax.map(lambda sample: fourier_layer(sample, shaped), field_all)
    outputs, pullback = jax.vjp(objective, fields, spectral)
    field_grad, spectral_grad = pullback(cotangent)
    return (outputs, field_grad, spectral_grad)
```

```python
import functools
import math

import jax
import jax.numpy as jnp
import numpy as np
from jax import lax
from jax.experimental import pallas as pl
from jax.experimental.pallas import tpu as pltpu
from jax.sharding import PartitionSpec as P

C = 20
NX, NY, NR = 4, 2, 512
GX, GY = 8, 16
S6 = 6
KX = 12
F32 = jnp.float32
EXACT = lax.Precision.HIGHEST
VMEM = pltpu.VMEM
INV_CELLS = 1.0 / (32 * 32 * 512)
INTERPRET = False


def freq(i, n):
    return i if i < n // 2 else i - n


def z_table():
    r = np.arange(NR)
    z, t = r // 8, r % 8
    out = np.zeros((S6, 2, GY, NR))
    for s in range(S6):
        for j in range(GY):
            m = 6 * j + s
            kz, kt = freq(m // 8, 12), freq(m % 8, 8)
            w = (kz * z * 8 + kt * t * 64) % 512
            ang = w * (2.0 * math.pi / 512)
            out[s, 0, j] = np.cos(ang)
            out[s, 1, j] = -np.sin(ang)
    return out.reshape(S6 * 2 * GY, NR).astype(np.float32)


def rot(k, n, sign):
    ang = ((k * n) % 32) * (2.0 * math.pi / 32)
    c, s = math.cos(ang), sign * math.sin(ang)
    return np.array([[c, -s], [s, c]])


def y_forward():
    out = np.zeros((2, 3, 8, NY, 2, GY))
    for t in range(3):
        for h in range(4):
            for yl in range(NY):
                for g in range(GY):
                    out[:, t, h, yl, :, g] = rot(freq(3 * h + t, 12), 2 * g + yl, -1)
    return out.reshape(48, 64).astype(np.float32)


def y_inverse():
    out = np.zeros((NY, 2, GY, 2, 3, 4))
    for t in range(3):
        for h in range(4):
            for yl in range(NY):
                for g in range(GY):
                    out[yl, :, g, :, t, h] = rot(freq(3 * h + t, 12), 2 * g + yl, 1)
    return out.reshape(64, 24).astype(np.float32)


def x_forward(scale):
    out = np.zeros((2, 16, GX, NX, 2))
    for k in range(KX):
        for g in range(GX):
            for xl in range(NX):
                out[:, k, g, xl, :] = rot(freq(k, 12), 4 * g + xl, -1)
    return (out * scale).reshape(32, 64).astype(np.float32)


def x_inverse(scale):
    out = np.zeros((GX, NX, 2, 2, 16))
    for k in range(KX):
        for g in range(GX):
            for xl in range(NX):
                out[g, xl, :, :, k] = rot(freq(k, 12), 4 * g + xl, 1)
    return (out * scale).reshape(64, 32).astype(np.float32)


def call(body, outs, *args, scratch=(), smem=(), flops=10**7, name=None):
    specs = [
        pl.BlockSpec(memory_space=pltpu.SMEM if i in smem else VMEM) for i in range(len(args))
    ]
    shapes = [jax.ShapeDtypeStruct(s, F32) for s in outs]
    nbytes = 4 * sum(math.prod(s) for s in outs) + sum(a.size * a.dtype.itemsize for a in args)
    got = pl.pallas_call(
        body,
        out_shape=shapes,
        in_specs=specs,
        out_specs=[pl.BlockSpec(memory_space=VMEM)] * len(outs),
        scratch_shapes=list(scratch),
        cost_estimate=pl.CostEstimate(flops=flops, bytes_accessed=nbytes, transcendentals=0),
        interpret=INTERPRET,
        name=name,
    )(*args)
    return got if len(outs) > 1 else got[0]


def dot(a, b):
    return jnp.dot(a, b, precision=EXACT, preferred_element_type=F32)


def lanes(rows):
    return lax.broadcasted_iota(jnp.int32, (rows, 128), 1)


def load_cells(ref, x, y):
    return jnp.concatenate(
        [ref[pl.ds(x * 8 + tile * 2 + y, C, stride=32), :] for tile in range(4)], axis=1
    )


def store_cells(ref, x, y, value):
    for tile in range(4):
        ref[pl.ds(x * 8 + tile * 2 + y, C, stride=32), :] = value[:, tile * 128 : tile * 128 + 128]


def emit_depth(table_ref, stage_ref, send_ref):
    modes = lax.dot_general(
        table_ref[...], stage_ref[...], (((1,), (1,)), ((), ())), precision=EXACT, preferred_element_type=F32
    )
    lane = lanes(GY)
    for y in range(NY):
        for x in range(NX):
            for part in range(2):
                total = jnp.zeros((GY, 128), F32)
                for s in range(S6):
                    at = (s * 2 + part) * GY
                    piece = modes[at : at + GY, y * 128 : y * 128 + 128]
                    shift = (20 * s - 32 * x) % 128
                    if shift:
                        piece = pltpu.roll(piece, shift, axis=1)
                    total = jnp.where((lane >= 20 * s) & (lane < 20 * s + 20), piece, total)
                send_ref[pl.ds(x * 4 + y * 2 + part, GY, stride=16), :] = total


def gather_depth(recv_ref, table_ref, modes_ref):
    lane = lanes(GY)
    for y in range(NY):
        for part in range(2):
            pieces = [recv_ref[pl.ds(x * 4 + y * 2 + part, GY, stride=16), :] for x in range(NX)]
            for s in range(S6):
                total = jnp.zeros((GY, 128), F32)
                for x in range(NX):
                    shift = (32 * x - 20 * s) % 128
                    piece = pltpu.roll(pieces[x], shift, axis=1) if shift else pieces[x]
                    total = jnp.where((lane >= 32 * x) & (lane < 32 * x + 20), piece, total)
                at = (s * 2 + part) * GY
                modes_ref[at : at + GY, y * 128 : y * 128 + 128] = total
    return lax.dot_general(
        modes_ref[...], table_ref[...], (((0,), (0,)), ((), ())), precision=EXACT, preferred_element_type=F32
    )


def depth_forward(fields_ref, table_ref, send_ref, stage_ref):
    stage_ref[...] = jnp.zeros_like(stage_ref)
    for y in range(NY):
        for x in range(NX):
            at = (y * NX + x) * 32
            stage_ref[at : at + C, :] = load_cells(fields_ref, x, y)
    emit_depth(table_ref, stage_ref, send_ref)


def bypass_fields(fields_ref, map_ref, out_ref):
    for y in range(NY):
        for x in range(NX):
            at = (y * NX + x) * 32
            out_ref[at : at + C, :] = dot(map_ref[...], load_cells(fields_ref, x, y))
            out_ref[at + C : at + 32, :] = jnp.zeros((32 - C, NR), F32)


def bypass_signal(signal_ref, map_ref, out_ref):
    for cell in range(8):
        at = cell * 32
        out_ref[at : at + C, :] = dot(map_ref[...], signal_ref[at : at + C, :])
        out_ref[at + C : at + 32, :] = jnp.zeros((32 - C, NR), F32)


def y_spectrum(recv_ref, table_ref, send_ref):
    columns = []
    for x in range(NX):
        columns.append(
            jnp.concatenate(
                [recv_ref[pl.ds(x * 4 + row, GY, stride=16), :] for row in range(4)], axis=0
            )
        )
    turned = dot(table_ref[...], jnp.concatenate(columns, axis=1))
    for x in range(NX):
        for part in range(2):
            row = x * 2 + part
            t0, t1, t2 = [
                turned[part * 24 + t * 8 : part * 24 + t * 8 + 8, x * 128 : x * 128 + 128] for t in range(3)
            ]
            send_ref[pl.ds(row, 4, stride=32), :] = t0[:4]
            send_ref[pl.ds(8 + row, 4, stride=32), :] = t1[:4]
            send_ref[pl.ds(16 + row, 4, stride=32), :] = t2[:4]
            send_ref[pl.ds(24 + row, 4, stride=32), :] = pltpu.roll(t1, 68, axis=1)[:4]


def y_cells(recv_ref, table_ref, send_ref, stage_ref):
    lane = lanes(4)
    for x in range(NX):
        for part in range(2):
            row = x * 2 + part
            t0, low, t2, high = [recv_ref[pl.ds(slot * 8 + row, 4, stride=32), :] for slot in range(4)]
            at = part * 12
            cut = slice(x * 128, x * 128 + 128)
            stage_ref[at : at + 4, cut] = t0
            stage_ref[at + 4 : at + 8, cut] = jnp.where(lane < 60, low, pltpu.roll(high, 60, axis=1))
            stage_ref[at + 8 : at + 12, cut] = t2
    cells = dot(table_ref[...], stage_ref[...])
    for x in range(NX):
        for row in range(4):
            send_ref[pl.ds(x * 4 + row, GY, stride=16), :] = cells[
                row * 16 : row * 16 + 16, x * 128 : x * 128 + 128
            ]


def x_spectrum(recv_ref, table_ref):
    found = []
    for tile in range(2):
        data = jnp.concatenate(
            [recv_ref[src * 16 + tile * 8 : src * 16 + tile * 8 + 8, :] for src in range(GX)], axis=0
        )
        found.append(dot(table_ref[...], data))
    return found


def slots(odd):
    for s in range(6):
        yield 0, s, s + 3 * odd
    for s in range(3):
        yield 1, s, s + 6 * (1 - odd)


def x_cells(mixed, table_ref, send_ref):
    for tile in range(2):
        cells = dot(table_ref[...], mixed[tile])
        for g in range(GX):
            send_ref[g * 16 + tile * 8 : g * 16 + tile * 8 + 8, :] = cells[g * 8 : g * 8 + 8, :]


def weight_row(pair, c):
    return pl.ds(pair * (KX * C) + c, KX, stride=C)


def x_mix(odd_ref, recv_ref, weight_ref, fwd_ref, inv_ref, send_ref, spec_ref, mixed_ref):
    odd = odd_ref[0]
    spectrum = x_spectrum(recv_ref, fwd_ref)
    for tile in range(2):
        spec_ref[tile * 32 : tile * 32 + 32, :] = spectrum[tile]
    mixed_ref[...] = jnp.zeros_like(mixed_ref)
    for tile, s, pair in slots(odd):
        real = spectrum[tile][:KX]
        imag = spectrum[tile][16 : 16 + KX]
        out_real = jnp.zeros((KX, C), F32)
        out_imag = jnp.zeros((KX, C), F32)
        for c in range(C):
            wr = weight_ref[weight_row(pair, c), :]
            wi = weight_ref[weight_row(9 + pair, c), :]
            at = 20 * s + c
            sr = real[:, at : at + 1]
            si = imag[:, at : at + 1]
            out_real = out_real + (sr * wr - si * wi)
            out_imag = out_imag + (sr * wi + si * wr)
        mixed_ref[tile * 32 : tile * 32 + KX, 20 * s : 20 * s + C] = out_real
        mixed_ref[tile * 32 + 16 : tile * 32 + 16 + KX, 20 * s : 20 * s + C] = out_imag
    x_cells([mixed_ref[:32, :], mixed_ref[32:, :]], inv_ref, send_ref)


def x_dual(recv_ref, spec_ref, fwd_ref, dual_ref, share_ref):
    spectrum = x_spectrum(recv_ref, fwd_ref)
    copies = share_ref.shape[0] // 128
    for tile in range(2):
        dual_ref[tile * 32 : tile * 32 + 32, :] = spectrum[tile]
        for n in range(copies):
            share_ref[n * 128 + tile * 32 : n * 128 + tile * 32 + 32, :] = spec_ref[
                tile * 32 : tile * 32 + 32, :
            ]
            share_ref[n * 128 + 64 + tile * 32 : n * 128 + 96 + tile * 32, :] = spectrum[tile]


def x_unmix(odd_ref, dual_ref, weight_ref, inv_ref, send_ref):
    odd = odd_ref[0]
    lane = lanes(KX)
    back = [[jnp.zeros((KX, 128), F32) for _ in range(2)] for _ in range(2)]
    for tile, s, pair in slots(odd):
        dr = dual_ref[tile * 32 : tile * 32 + KX, 20 * s : 20 * s + C]
        di = dual_ref[tile * 32 + 16 : tile * 32 + 16 + KX, 20 * s : 20 * s + C]
        for c in range(C):
            wr = weight_ref[weight_row(pair, c), :]
            wi = weight_ref[weight_row(9 + pair, c), :]
            real = jnp.sum(dr * wr + di * wi, axis=1, keepdims=True)
            imag = jnp.sum(di * wr - dr * wi, axis=1, keepdims=True)
            here = lane == 20 * s + c
            back[tile][0] = jnp.where(here, real, back[tile][0])
            back[tile][1] = jnp.where(here, imag, back[tile][1])
    gap = jnp.zeros((16 - KX, 128), F32)
    x_cells(
        [jnp.concatenate([re, gap, im, gap], axis=0) for re, im in back], inv_ref, send_ref
    )


def weight_grad(odd_ref, share_ref, grad_ref):
    odd = odd_ref[0]
    samples = share_ref.shape[0] // 128
    for tile, s, pair in slots(odd):
        spec, dual = [], []
        for n in range(samples):
            at = n * 128 + tile * 32
            spec.append([share_ref[at + p * 16 : at + p * 16 + KX, :] for p in range(2)])
            dual.append(
                [share_ref[at + 64 + p * 16 : at + 64 + p * 16 + KX, 20 * s : 20 * s + C] for p in range(2)]
            )
        for c in range(C):
            real = jnp.zeros((KX, C), F32)
            imag = jnp.zeros((KX, C), F32)
            at = 20 * s + c
            for n in range(samples):
                sr = spec[n][0][:, at : at + 1]
                si = spec[n][1][:, at : at + 1]
                dr, di = dual[n]
                real = real + (sr * dr + si * di)
                imag = imag + (sr * di - si * dr)
            grad_ref[weight_row(pair, c), :] = real
            grad_ref[weight_row(9 + pair, c), :] = imag


def activate(recv_ref, table_ref, bypass_ref, cotangent_ref, out_ref, signal_ref, send_ref, modes_ref):
    spectral = gather_depth(recv_ref, table_ref, modes_ref)
    k = math.sqrt(2.0 / math.pi)
    for y in range(NY):
        for x in range(NX):
            at = (y * NX + x) * 32
            v = spectral[at : at + C, :] + bypass_ref[at : at + C, :]
            cube = v * v * v
            th = jnp.tanh(k * (v + 0.044715 * cube))
            half = 0.5 * (1.0 + th)
            store_cells(out_ref, x, y, v * half)
            slope = half + 0.5 * v * (1.0 - th * th) * (k * (1.0 + 3 * 0.044715 * (v * v)))
            signal_ref[at : at + C, :] = slope * load_cells(cotangent_ref, x, y)
            signal_ref[at + C : at + 32, :] = jnp.zeros((32 - C, NR), F32)
    emit_depth(table_ref, signal_ref, send_ref)


def finish(recv_ref, table_ref, bypass_ref, out_ref, modes_ref):
    spectral = gather_depth(recv_ref, table_ref, modes_ref)
    for y in range(NY):
        for x in range(NX):
            at = (y * NX + x) * 32
            store_cells(out_ref, x, y, spectral[at : at + C, :] + bypass_ref[at : at + C, :])


def as_rows(a):
    return a.reshape(C * NX, NY, 4, 128).transpose(0, 2, 1, 3).reshape(640, 128)


def from_rows(a):
    return a.reshape(C * NX, 4, NY, 128).transpose(0, 2, 1, 3).reshape(1, C, NX, NY, NR)


CELLS = (256, NR)
SEND_Y = (GY * 16, 128)
SEND_X = (GX * 16, 128)


def stages(samples):
    tz, ay, by = z_table(), y_forward(), y_inverse()
    ax, bx = x_forward(1.0), x_inverse(INV_CELLS)
    ax_dual, bx_dual = x_forward(INV_CELLS), x_inverse(1.0)
    modes = [VMEM((192, 256), F32)]
    return dict(
        depth_forward=lambda f: call(depth_forward, [SEND_Y], f, tz, scratch=[VMEM(CELLS, F32)], name="depth_forward"),
        bypass_fields=lambda f, b: call(bypass_fields, [CELLS], f, b, name="bypass_fields"),
        bypass_signal=lambda f, b: call(bypass_signal, [CELLS], f, b, name="bypass_signal"),
        y_spectrum=lambda r: call(y_spectrum, [SEND_X], r, ay, name="y_spectrum"),
        y_cells=lambda r: call(y_cells, [SEND_Y], r, by, scratch=[VMEM((24, 512), F32)], name="y_cells"),
        x_mix=lambda o, r, w: call(
            x_mix, [SEND_X, (64, 128)], o, r, w, ax, bx, scratch=[VMEM((64, 128), F32)], smem=(0,), name="x_mix"
        ),
        x_dual=lambda r, s: call(x_dual, [(64, 128), (samples * 128, 128)], r, s, ax_dual, name="x_dual"),
        x_unmix=lambda o, d, w: call(x_unmix, [SEND_X], o, d, w, bx_dual, smem=(0,), name="x_unmix"),
        weight_grad=lambda o, s: call(weight_grad, [(2 * 9 * KX * C, C)], o, s, smem=(0,), name="weight_grad"),
        activate=lambda r, b, ct: call(
            activate, [(640, 128), CELLS, SEND_Y], r, tz, b, ct, scratch=modes, name="activate"
        ),
        finish=lambda r, b: call(finish, [(640, 128)], r, tz, b, scratch=modes, name="finish"),
    )


def swap(a, axis, n):
    rows = a.shape[0] // n
    return lax.all_to_all(
        a.reshape(n, rows, 128), axis, split_axis=0, concat_axis=0, tiled=True
    ).reshape(n * rows, 128)


def on_device(fields, cotangent, spectral, bypass):
    samples = lax.axis_size("dp")
    st = stages(samples)
    odd = (lax.axis_index("gx") % 2).astype(jnp.int32).reshape(1)
    rows = as_rows(fields)
    weights = spectral.reshape(2 * 9 * KX * C, C)
    to_y = functools.partial(swap, axis="gy", n=GY)
    to_x = functools.partial(swap, axis="gx", n=GX)
    direct = st["bypass_fields"](rows, bypass.T)
    arrived = to_x(st["y_spectrum"](to_y(st["depth_forward"](rows))))
    mixed, spec = st["x_mix"](odd, arrived, weights)
    arrived = to_y(st["y_cells"](to_x(mixed)))
    output, signal, sent = st["activate"](arrived, direct, as_rows(cotangent))
    direct = st["bypass_signal"](signal, bypass)
    arrived = to_x(st["y_spectrum"](to_y(sent)))
    dual, share = st["x_dual"](arrived, spec)
    shared = swap(share, "dp", samples)
    grad = st["weight_grad"](odd, shared)
    arrived = to_y(st["y_cells"](to_x(st["x_unmix"](odd, dual, weights))))
    field_grad = st["finish"](arrived, direct)
    return (from_rows(output), from_rows(field_grad), grad.reshape(spectral.shape))


def solution(mesh):
    cells = P("dp", None, "gx", "gy", None)
    modes = P(None, "gx", "gy", None, None, None)
    return jax.shard_map(
        on_device,
        mesh=mesh,
        in_specs=(cells, cells, modes, P()),
        out_specs=(cells, cells, modes),
        check_vma=False,
    )
```

```python
import functools
import math

import jax
import jax.numpy as jnp
import numpy as np
from jax import lax
from jax.experimental import pallas as pl
from jax.experimental.pallas import tpu as pltpu
from jax.sharding import PartitionSpec as P

C = 20
NX, NY, NR = 4, 2, 512
GX, GY = 8, 16
S6 = 6
KX = 12
F32 = jnp.float32
EXACT = lax.Precision.HIGHEST
VMEM = pltpu.VMEM
INV_CELLS = 1.0 / (32 * 32 * 512)
INTERPRET = False


def freq(i, n):
    return i if i < n // 2 else i - n


def z_table():
    r = np.arange(NR)
    z, t = r // 8, r % 8
    out = np.zeros((S6, 2, GY, NR))
    for s in range(S6):
        for j in range(GY):
            m = 6 * j + s
            kz, kt = freq(m // 8, 12), freq(m % 8, 8)
            w = (kz * z * 8 + kt * t * 64) % 512
            ang = w * (2.0 * math.pi / 512)
            out[s, 0, j] = np.cos(ang)
            out[s, 1, j] = -np.sin(ang)
    return out.reshape(S6 * 2 * GY, NR).astype(np.float32)


def rot(k, n, sign):
    ang = ((k * n) % 32) * (2.0 * math.pi / 32)
    c, s = math.cos(ang), sign * math.sin(ang)
    return np.array([[c, -s], [s, c]])


def y_forward():
    out = np.zeros((2, 3, 8, NY, 2, GY))
    for t in range(3):
        for h in range(4):
            for yl in range(NY):
                for g in range(GY):
                    out[:, t, h, yl, :, g] = rot(freq(3 * h + t, 12), 2 * g + yl, -1)
    return out.reshape(48, 64).astype(np.float32)


def y_inverse():
    out = np.zeros((NY, 2, GY, 2, 3, 4))
    for t in range(3):
        for h in range(4):
            for yl in range(NY):
                for g in range(GY):
                    out[yl, :, g, :, t, h] = rot(freq(3 * h + t, 12), 2 * g + yl, 1)
    return out.reshape(64, 24).astype(np.float32)


def x_forward(scale):
    out = np.zeros((2, 16, GX, NX, 2))
    for k in range(KX):
        for g in range(GX):
            for xl in range(NX):
                out[:, k, g, xl, :] = rot(freq(k, 12), 4 * g + xl, -1)
    return (out * scale).reshape(32, 64).astype(np.float32)


def x_inverse(scale):
    out = np.zeros((GX, NX, 2, 2, 16))
    for k in range(KX):
        for g in range(GX):
            for xl in range(NX):
                out[g, xl, :, :, k] = rot(freq(k, 12), 4 * g + xl, 1)
    return (out * scale).reshape(64, 32).astype(np.float32)


def call(body, outs, *args, scratch=(), smem=(), flops=10**7, name=None):
    specs = [
        pl.BlockSpec(memory_space=pltpu.SMEM if i in smem else VMEM) for i in range(len(args))
    ]
    shapes = [jax.ShapeDtypeStruct(s, F32) for s in outs]
    nbytes = 4 * sum(math.prod(s) for s in outs) + sum(a.size * a.dtype.itemsize for a in args)
    got = pl.pallas_call(
        body,
        out_shape=shapes,
        in_specs=specs,
        out_specs=[pl.BlockSpec(memory_space=VMEM)] * len(outs),
        scratch_shapes=list(scratch),
        compiler_params=pltpu.CompilerParams(vmem_limit_bytes=16 << 20),
        cost_estimate=pl.CostEstimate(flops=flops, bytes_accessed=nbytes, transcendentals=0),
        interpret=INTERPRET,
        name=name,
    )(*args)
    return got if len(outs) > 1 else got[0]


def dot(a, b):
    return jnp.dot(a, b, precision=EXACT, preferred_element_type=F32)


def lanes(rows):
    return lax.broadcasted_iota(jnp.int32, (rows, 128), 1)


def load_cells(ref, x, y):
    return jnp.concatenate(
        [ref[pl.ds(x * 8 + tile * 2 + y, C, stride=32), :] for tile in range(4)], axis=1
    )


def store_cells(ref, x, y, value):
    for tile in range(4):
        ref[pl.ds(x * 8 + tile * 2 + y, C, stride=32), :] = value[:, tile * 128 : tile * 128 + 128]


def emit_depth(table_ref, stage_ref, send_ref):
    modes = lax.dot_general(
        table_ref[...], stage_ref[...], (((1,), (1,)), ((), ())), precision=EXACT, preferred_element_type=F32
    )
    lane = lanes(GY)
    for y in range(NY):
        for x in range(NX):
            for part in range(2):
                total = jnp.zeros((GY, 128), F32)
                for s in range(S6):
                    at = (s * 2 + part) * GY
                    piece = modes[at : at + GY, y * 128 : y * 128 + 128]
                    shift = (20 * s - 32 * x) % 128
                    if shift:
                        piece = pltpu.roll(piece, shift, axis=1)
                    total = jnp.where((lane >= 20 * s) & (lane < 20 * s + 20), piece, total)
                send_ref[pl.ds(x * 4 + y * 2 + part, GY, stride=16), :] = total


def gather_depth(recv_ref, table_ref, modes_ref):
    lane = lanes(GY)
    for y in range(NY):
        for part in range(2):
            pieces = [recv_ref[pl.ds(x * 4 + y * 2 + part, GY, stride=16), :] for x in range(NX)]
            for s in range(S6):
                total = jnp.zeros((GY, 128), F32)
                for x in range(NX):
                    shift = (32 * x - 20 * s) % 128
                    piece = pltpu.roll(pieces[x], shift, axis=1) if shift else pieces[x]
                    total = jnp.where((lane >= 32 * x) & (lane < 32 * x + 20), piece, total)
                at = (s * 2 + part) * GY
                modes_ref[at : at + GY, y * 128 : y * 128 + 128] = total
    return lax.dot_general(
        modes_ref[...], table_ref[...], (((0,), (0,)), ((), ())), precision=EXACT, preferred_element_type=F32
    )


def depth_forward(fields_ref, table_ref, send_ref, stage_ref):
    stage_ref[...] = jnp.zeros_like(stage_ref)
    for y in range(NY):
        for x in range(NX):
            at = (y * NX + x) * 32
            stage_ref[at : at + C, :] = load_cells(fields_ref, x, y)
    emit_depth(table_ref, stage_ref, send_ref)


def bypass_fields(fields_ref, map_ref, out_ref):
    for y in range(NY):
        for x in range(NX):
            at = (y * NX + x) * 32
            out_ref[at : at + C, :] = dot(map_ref[...], load_cells(fields_ref, x, y))
            out_ref[at + C : at + 32, :] = jnp.zeros((32 - C, NR), F32)


def bypass_signal(signal_ref, map_ref, out_ref):
    for cell in range(8):
        at = cell * 32
        out_ref[at : at + C, :] = dot(map_ref[...], signal_ref[at : at + C, :])
        out_ref[at + C : at + 32, :] = jnp.zeros((32 - C, NR), F32)


def y_spectrum(recv_ref, table_ref, send_ref):
    columns = []
    for x in range(NX):
        columns.append(
            jnp.concatenate(
                [recv_ref[pl.ds(x * 4 + row, GY, stride=16), :] for row in range(4)], axis=0
            )
        )
    turned = dot(table_ref[...], jnp.concatenate(columns, axis=1))
    for x in range(NX):
        for part in range(2):
            row = x * 2 + part
            t0, t1, t2 = [
                turned[part * 24 + t * 8 : part * 24 + t * 8 + 8, x * 128 : x * 128 + 128] for t in range(3)
            ]
            send_ref[pl.ds(row, 4, stride=32), :] = t0[:4]
            send_ref[pl.ds(8 + row, 4, stride=32), :] = t1[:4]
            send_ref[pl.ds(16 + row, 4, stride=32), :] = t2[:4]
            send_ref[pl.ds(24 + row, 4, stride=32), :] = pltpu.roll(t1, 68, axis=1)[:4]


def y_cells(recv_ref, table_ref, send_ref, stage_ref):
    lane = lanes(4)
    for x in range(NX):
        for part in range(2):
            row = x * 2 + part
            t0, low, t2, high = [recv_ref[pl.ds(slot * 8 + row, 4, stride=32), :] for slot in range(4)]
            at = part * 12
            cut = slice(x * 128, x * 128 + 128)
            stage_ref[at : at + 4, cut] = t0
            stage_ref[at + 4 : at + 8, cut] = jnp.where(lane < 60, low, pltpu.roll(high, 60, axis=1))
            stage_ref[at + 8 : at + 12, cut] = t2
    cells = dot(table_ref[...], stage_ref[...])
    for x in range(NX):
        for row in range(4):
            send_ref[pl.ds(x * 4 + row, GY, stride=16), :] = cells[
                row * 16 : row * 16 + 16, x * 128 : x * 128 + 128
            ]


def x_spectrum(recv_ref, table_ref):
    found = []
    for tile in range(2):
        data = jnp.concatenate(
            [recv_ref[src * 16 + tile * 8 : src * 16 + tile * 8 + 8, :] for src in range(GX)], axis=0
        )
        found.append(dot(table_ref[...], data))
    return found


def slots(odd):
    for s in range(6):
        yield 0, s, s + 3 * odd
    for s in range(3):
        yield 1, s, s + 6 * (1 - odd)


def x_cells(mixed, table_ref, send_ref):
    for tile in range(2):
        cells = dot(table_ref[...], mixed[tile])
        for g in range(GX):
            send_ref[g * 16 + tile * 8 : g * 16 + tile * 8 + 8, :] = cells[g * 8 : g * 8 + 8, :]


def weight_row(pair, c):
    return pl.ds(pair * (KX * C) + c, KX, stride=C)


def packed_row(part, c, tile):
    at = ((part * C + c) * 2 + tile) * 16
    return slice(at, at + 16)


def pack_weights(odd_ref, weight_ref, packed_ref):
    odd = odd_ref[0]
    packed_ref[...] = jnp.zeros_like(packed_ref)
    for tile, s, pair in slots(odd):
        for part in range(2):
            for c in range(C):
                at = packed_row(part, c, tile).start
                packed_ref[at : at + KX, 20 * s : 20 * s + C] = weight_ref[weight_row(9 * part + pair, c), :]


def group_start():
    lane = lanes(16)
    return jnp.right_shift(lane * 205, 12) * 20


def pick(a, index):
    return jnp.take_along_axis(a, index, axis=1, mode="promise_in_bounds")


def x_mix(recv_ref, packed_ref, fwd_ref, inv_ref, send_ref, spec_ref):
    spectrum = x_spectrum(recv_ref, fwd_ref)
    start = group_start()
    mixed = []
    for tile in range(2):
        spec_ref[tile * 32 : tile * 32 + 32, :] = spectrum[tile]
        real, imag = spectrum[tile][:16], spectrum[tile][16:]
        out_real = jnp.zeros((16, 128), F32)
        out_imag = jnp.zeros((16, 128), F32)
        for c in range(C):
            index = jnp.minimum(start + c, 127)
            sr, si = pick(real, index), pick(imag, index)
            wr = packed_ref[packed_row(0, c, tile), :]
            wi = packed_ref[packed_row(1, c, tile), :]
            out_real = out_real + (sr * wr - si * wi)
            out_imag = out_imag + (sr * wi + si * wr)
        mixed.append(jnp.concatenate([out_real, out_imag], axis=0))
    x_cells(mixed, inv_ref, send_ref)


def x_unmix(recv_ref, spec_ref, packed_ref, fwd_ref, inv_ref, sum_ref, share_ref, send_ref, high_ref, low_ref):
    spectrum = x_spectrum(recv_ref, fwd_ref)
    copies = share_ref.shape[0] // 128
    for tile in range(2):
        for n in range(copies):
            at = n * 128 + tile * 32
            share_ref[at : at + 32, :] = spec_ref[tile * 32 : tile * 32 + 32, :]
            share_ref[at + 64 : at + 96, :] = spectrum[tile]
        dr, di = spectrum[tile][:16], spectrum[tile][16:]
        for c in range(C):
            wr = packed_ref[packed_row(0, c, tile), :]
            wi = packed_ref[packed_row(1, c, tile), :]
            for part, term in enumerate((dr * wr + di * wi, di * wr - dr * wi)):
                high = term.astype(jnp.bfloat16)
                at = (tile * 2 + part) * 16
                high_ref[at : at + 16, c * 128 : c * 128 + 128] = high
                low_ref[at : at + 16, c * 128 : c * 128 + 128] = (term - high.astype(F32)).astype(jnp.bfloat16)
    back = jnp.dot(high_ref[...], sum_ref[...], preferred_element_type=F32) + jnp.dot(
        low_ref[...], sum_ref[...], preferred_element_type=F32
    )
    x_cells([back[:32], back[32:]], inv_ref, send_ref)


def sum_table():
    out = np.zeros((C, 128, 128))
    for c in range(C):
        for s in range(6):
            out[c, 20 * s : 20 * s + C, 20 * s + c] = 1.0
    return out.reshape(C * 128, 128).astype(jnp.bfloat16)


def weight_grad(odd_ref, share_ref, grad_ref):
    odd = odd_ref[0]
    samples = share_ref.shape[0] // 128
    start = group_start()
    owned = list(slots(odd))
    for tile in range(2):
        spec, dual = [], []
        for n in range(samples):
            at = n * 128 + tile * 32
            spec.append([share_ref[at + p * 16 : at + p * 16 + 16, :] for p in range(2)])
            dual.append([share_ref[at + 64 + p * 16 : at + 80 + p * 16, :] for p in range(2)])
        for c in range(C):
            index = jnp.minimum(start + c, 127)
            real = jnp.zeros((16, 128), F32)
            imag = jnp.zeros((16, 128), F32)
            for n in range(samples):
                sr, si = pick(spec[n][0], index), pick(spec[n][1], index)
                dr, di = dual[n]
                real = real + (sr * dr + si * di)
                imag = imag + (sr * di - si * dr)
            for where, s, pair in owned:
                if where == tile:
                    grad_ref[weight_row(pair, c), :] = real[:KX, 20 * s : 20 * s + C]
                    grad_ref[weight_row(9 + pair, c), :] = imag[:KX, 20 * s : 20 * s + C]


def activate(recv_ref, table_ref, bypass_ref, cotangent_ref, out_ref, signal_ref, send_ref, modes_ref):
    spectral = gather_depth(recv_ref, table_ref, modes_ref)
    k = math.sqrt(2.0 / math.pi)
    for y in range(NY):
        for x in range(NX):
            at = (y * NX + x) * 32
            v = spectral[at : at + C, :] + bypass_ref[at : at + C, :]
            cube = v * v * v
            th = jnp.tanh(k * (v + 0.044715 * cube))
            half = 0.5 * (1.0 + th)
            store_cells(out_ref, x, y, v * half)
            slope = half + 0.5 * v * (1.0 - th * th) * (k * (1.0 + 3 * 0.044715 * (v * v)))
            signal_ref[at : at + C, :] = slope * load_cells(cotangent_ref, x, y)
            signal_ref[at + C : at + 32, :] = jnp.zeros((32 - C, NR), F32)
    emit_depth(table_ref, signal_ref, send_ref)


def finish(recv_ref, table_ref, bypass_ref, out_ref, modes_ref):
    spectral = gather_depth(recv_ref, table_ref, modes_ref)
    for y in range(NY):
        for x in range(NX):
            at = (y * NX + x) * 32
            store_cells(out_ref, x, y, spectral[at : at + C, :] + bypass_ref[at : at + C, :])


def as_rows(a):
    return a.reshape(C * NX, NY, 4, 128).transpose(0, 2, 1, 3).reshape(640, 128)


def from_rows(a):
    return a.reshape(C * NX, 4, NY, 128).transpose(0, 2, 1, 3).reshape(1, C, NX, NY, NR)


CELLS = (256, NR)
SEND_Y = (GY * 16, 128)
SEND_X = (GX * 16, 128)
PACKED = (2 * C * 2 * 16, 128)


def stages(samples):
    tz, ay, by = z_table(), y_forward(), y_inverse()
    ax, bx = x_forward(1.0), x_inverse(INV_CELLS)
    ax_dual, bx_dual = x_forward(INV_CELLS), x_inverse(1.0)
    modes = [VMEM((192, 256), F32)]
    return dict(
        depth_forward=lambda f: call(depth_forward, [SEND_Y], f, tz, scratch=[VMEM(CELLS, F32)], name="depth_forward"),
        bypass_fields=lambda f, b: call(bypass_fields, [CELLS], f, b, name="bypass_fields"),
        bypass_signal=lambda f, b: call(bypass_signal, [CELLS], f, b, name="bypass_signal"),
        y_spectrum=lambda r: call(y_spectrum, [SEND_X], r, ay, name="y_spectrum"),
        y_cells=lambda r: call(y_cells, [SEND_Y], r, by, scratch=[VMEM((24, 512), F32)], name="y_cells"),
        pack_weights=lambda o, w: call(pack_weights, [PACKED], o, w, smem=(0,), name="pack_weights"),
        x_mix=lambda r, w: call(x_mix, [SEND_X, (64, 128)], r, w, ax, bx, name="x_mix"),
        x_unmix=lambda r, s, w: call(
            x_unmix,
            [(samples * 128, 128), SEND_X],
            *(r, s, w, ax_dual, bx_dual, sum_table()),
            scratch=[VMEM((64, C * 128), jnp.bfloat16)] * 2,
            name="x_unmix",
        ),
        weight_grad=lambda o, s: call(weight_grad, [(2 * 9 * KX * C, C)], o, s, smem=(0,), name="weight_grad"),
        activate=lambda r, b, ct: call(
            activate, [(640, 128), CELLS, SEND_Y], r, tz, b, ct, scratch=modes, name="activate"
        ),
        finish=lambda r, b: call(finish, [(640, 128)], r, tz, b, scratch=modes, name="finish"),
    )


def swap(a, axis, n):
    rows = a.shape[0] // n
    return lax.all_to_all(
        a.reshape(n, rows, 128), axis, split_axis=0, concat_axis=0, tiled=True
    ).reshape(n * rows, 128)


def on_device(fields, cotangent, spectral, bypass):
    samples = lax.axis_size("dp")
    st = stages(samples)
    odd = (lax.axis_index("gx") % 2).astype(jnp.int32).reshape(1)
    rows = as_rows(fields)
    weights = spectral.reshape(2 * 9 * KX * C, C)
    to_y = functools.partial(swap, axis="gy", n=GY)
    to_x = functools.partial(swap, axis="gx", n=GX)
    direct = st["bypass_fields"](rows, bypass.T)
    arrived = to_x(st["y_spectrum"](to_y(st["depth_forward"](rows))))
    packed = st["pack_weights"](odd, weights)
    mixed, spec = st["x_mix"](arrived, packed)
    arrived = to_y(st["y_cells"](to_x(mixed)))
    output, signal, sent = st["activate"](arrived, direct, as_rows(cotangent))
    direct = st["bypass_signal"](signal, bypass)
    arrived = to_x(st["y_spectrum"](to_y(sent)))
    share, sent = st["x_unmix"](arrived, spec, packed)
    shared = swap(share, "dp", samples)
    grad = st["weight_grad"](odd, shared)
    arrived = to_y(st["y_cells"](to_x(sent)))
    field_grad = st["finish"](arrived, direct)
    return (from_rows(output), from_rows(field_grad), grad.reshape(spectral.shape))


def solution(mesh):
    cells = P("dp", None, "gx", "gy", None)
    modes = P(None, "gx", "gy", None, None, None)
    return jax.shard_map(
        on_device,
        mesh=mesh,
        in_specs=(cells, cells, modes, P()),
        out_specs=(cells, cells, modes),
        check_vma=False,
    )
```

```python
import functools
import math

import jax
import jax.numpy as jnp
import numpy as np
from jax import lax
from jax.experimental import pallas as pl
from jax.experimental.pallas import tpu as pltpu
from jax.sharding import PartitionSpec as P


C = 20
NX, NY, NR = 4, 2, 512
GX, GY = 8, 16
S6 = 6
KX = 12
F32 = jnp.float32
VMEM = pltpu.VMEM
INV_CELLS = 1.0 / (32 * 32 * 512)
INTERPRET = False


def freq(i, n):
    return i if i < n // 2 else i - n


def z_table():
    r = np.arange(NR)
    z, t = r // 8, r % 8
    out = np.zeros((S6, 2, GY, NR))
    for s in range(S6):
        for j in range(GY):
            m = 6 * j + s
            kz, kt = freq(m // 8, 12), freq(m % 8, 8)
            w = (kz * z * 8 + kt * t * 64) % 512
            ang = w * (2.0 * math.pi / 512)
            out[s, 0, j] = np.cos(ang)
            out[s, 1, j] = -np.sin(ang)
    return out.reshape(S6 * 2 * GY, NR).astype(np.float32)


def split_table(table, axis):
    high = table.astype(jnp.bfloat16)
    low = (table - high.astype(np.float32)).astype(jnp.bfloat16)
    return np.concatenate([high, low], axis=axis)


COS = [(-1) ** i * math.pi ** (2 * i) / math.factorial(2 * i) for i in range(11)]
SIN = [(-1) ** i * math.pi ** (2 * i + 1) / math.factorial(2 * i + 1) for i in range(11)]


def rotation(mode, cell, part_out, part_in, sign, scale):
    k = jnp.where(mode >= 6, mode - 12, mode)
    turns = (((k * cell + 16) & 31) - 16).astype(F32) * (1.0 / 16)
    u = turns * turns
    cos = jnp.full_like(u, COS[-1])
    sin = jnp.full_like(u, SIN[-1])
    for i in range(len(COS) - 2, -1, -1):
        cos = cos * u + COS[i]
        sin = sin * u + SIN[i]
    sin = sin * turns * sign
    value = jnp.where(part_out == part_in, cos, jnp.where(part_out == 1, sin, -sin))
    return value * scale if scale != 1.0 else value


def row_col(rows, cols):
    shape = (rows, cols)
    return lax.broadcasted_iota(jnp.int32, shape, 0), lax.broadcasted_iota(jnp.int32, shape, 1)


def y_forward():
    row, col = row_col(48, 64)
    part = (row >= 24).astype(jnp.int32)
    rest = row - 24 * part
    mode = 3 * (rest & 7) + (rest >> 3)
    return rotation(mode, 2 * (col & 15) + (col >> 5), part, (col >> 4) & 1, -1.0, 1.0)


def y_inverse():
    row, col = row_col(64, 24)
    part = (col >= 12).astype(jnp.int32)
    rest = col - 12 * part
    mode = 3 * (rest & 3) + (rest >> 2)
    return rotation(mode, 2 * (row & 15) + (row >> 5), (row >> 4) & 1, part, 1.0, 1.0)


def x_forward(scale):
    row, col = row_col(32, 64)
    return rotation(row & 15, col >> 1, row >> 4, col & 1, -1.0, scale)


def x_inverse(scale):
    row, col = row_col(64, 32)
    return rotation(col & 15, row >> 1, row & 1, col >> 4, 1.0, scale)


def call(body, outs, *args, scratch=(), smem=(), hbm=(), vmem=16 << 20, flops=10**7):
    specs = [
        pl.BlockSpec(memory_space=pltpu.SMEM if i in smem else pltpu.HBM if i in hbm else VMEM)
        for i in range(len(args))
    ]
    shapes = [jax.ShapeDtypeStruct(s, F32) for s in outs]
    nbytes = 4 * sum(math.prod(s) for s in outs) + sum(a.size * a.dtype.itemsize for a in args)
    got = pl.pallas_call(
        body,
        out_shape=shapes,
        in_specs=specs,
        out_specs=[pl.BlockSpec(memory_space=VMEM)] * len(outs),
        scratch_shapes=list(scratch),
        compiler_params=pltpu.CompilerParams(vmem_limit_bytes=vmem),
        cost_estimate=pl.CostEstimate(flops=flops, bytes_accessed=nbytes, transcendentals=0),
        interpret=INTERPRET,
    )(*args)
    return got if len(outs) > 1 else got[0]


def halves(a):
    high = a.astype(jnp.bfloat16)
    return high, (a - high.astype(F32)).astype(jnp.bfloat16)


def dot(a, b, dims=((1,), (0,))):
    ah, al = a if isinstance(a, tuple) else halves(a)
    bh, bl = b if isinstance(b, tuple) else halves(b)

    def one(x, y):
        return lax.dot_general(x, y, (dims, ((), ())), preferred_element_type=F32)

    return one(ah, bh) + (one(ah, bl) + one(al, bh))


def pair(ref):
    rows = ref.shape[0] // 2
    return ref[:rows, :], ref[rows:, :]


def lanes(rows):
    return lax.broadcasted_iota(jnp.int32, (rows, 128), 1)


def load_cells(ref, x, y):
    return jnp.concatenate(
        [ref[pl.ds(x * 8 + tile * 2 + y, C, stride=32), :] for tile in range(4)], axis=1
    )


def store_cells(ref, x, y, value):
    for tile in range(4):
        ref[pl.ds(x * 8 + tile * 2 + y, C, stride=32), :] = value[:, tile * 128 : tile * 128 + 128]


def emit_depth(modes, send_ref):
    lane = lanes(GY)
    for y in range(NY):
        for x in range(NX):
            for part in range(2):
                total = jnp.zeros((GY, 128), F32)
                for s in range(S6):
                    at = (s * 2 + part) * GY
                    piece = modes[at : at + GY, y * 128 : y * 128 + 128]
                    shift = (20 * s - 32 * x) % 128
                    if shift:
                        piece = pltpu.roll(piece, shift, axis=1)
                    total = jnp.where((lane >= 20 * s) & (lane < 20 * s + 20), piece, total)
                send_ref[pl.ds(x * 4 + y * 2 + part, GY, stride=16), :] = total


def gather_depth(recv_ref, modes_ref):
    lane = lanes(GY)
    for y in range(NY):
        for part in range(2):
            pieces = [recv_ref[pl.ds(x * 4 + y * 2 + part, GY, stride=16), :] for x in range(NX)]
            for s in range(S6):
                total = jnp.zeros((GY, 128), F32)
                for x in range(NX):
                    shift = (32 * x - 20 * s) % 128
                    piece = pltpu.roll(pieces[x], shift, axis=1) if shift else pieces[x]
                    total = jnp.where((lane >= 32 * x) & (lane < 32 * x + 20), piece, total)
                at = (s * 2 + part) * GY
                modes_ref[at : at + GY, y * 128 : y * 128 + 128] = total
    return modes_ref[...]


def cell_rows():
    for y in range(NY):
        for x in range(NX):
            yield x, y, (y * NX + x) * 32


def depth_forward(fields_hbm, table_hbm, send_ref, fields_ref, table_ref, stage_ref, sems):
    fields_copy = pltpu.make_async_copy(fields_hbm, fields_ref, sems.at[0])
    table_copy = pltpu.make_async_copy(table_hbm, table_ref, sems.at[1])
    fields_copy.start()
    table_copy.start()
    stage_ref[...] = jnp.zeros_like(stage_ref)
    fields_copy.wait()
    for x, y, at in cell_rows():
        stage_ref[at : at + C, :] = load_cells(fields_ref, x, y)
    table_copy.wait()
    emit_depth(dot(pair(table_ref), stage_ref[...], ((1,), (1,))), send_ref)


def y_spectrum(recv_ref, send_ref):
    columns = []
    for x in range(NX):
        columns.append(
            jnp.concatenate(
                [recv_ref[pl.ds(x * 4 + row, GY, stride=16), :] for row in range(4)], axis=0
            )
        )
    turned = dot(y_forward(), jnp.concatenate(columns, axis=1))
    for x in range(NX):
        for part in range(2):
            row = x * 2 + part
            t0, t1, t2 = [
                turned[part * 24 + t * 8 : part * 24 + t * 8 + 8, x * 128 : x * 128 + 128] for t in range(3)
            ]
            send_ref[pl.ds(row, 4, stride=32), :] = t0[:4]
            send_ref[pl.ds(8 + row, 4, stride=32), :] = t1[:4]
            send_ref[pl.ds(16 + row, 4, stride=32), :] = t2[:4]
            send_ref[pl.ds(24 + row, 4, stride=32), :] = pltpu.roll(t1, 68, axis=1)[:4]


def y_cells(recv_ref, send_ref, stage_ref):
    lane = lanes(4)
    for x in range(NX):
        for part in range(2):
            row = x * 2 + part
            t0, low, t2, high = [recv_ref[pl.ds(slot * 8 + row, 4, stride=32), :] for slot in range(4)]
            at = part * 12
            cut = slice(x * 128, x * 128 + 128)
            stage_ref[at : at + 4, cut] = t0
            stage_ref[at + 4 : at + 8, cut] = jnp.where(lane < 60, low, pltpu.roll(high, 60, axis=1))
            stage_ref[at + 8 : at + 12, cut] = t2
    cells = dot(y_inverse(), stage_ref[...])
    for x in range(NX):
        for row in range(4):
            send_ref[pl.ds(x * 4 + row, GY, stride=16), :] = cells[
                row * 16 : row * 16 + 16, x * 128 : x * 128 + 128
            ]


def x_spectrum(recv_ref, scale):
    found = []
    table = halves(x_forward(scale))
    for tile in range(2):
        data = jnp.concatenate(
            [recv_ref[src * 16 + tile * 8 : src * 16 + tile * 8 + 8, :] for src in range(GX)], axis=0
        )
        found.append(dot(table, data))
    return found


def slots(odd):
    for s in range(6):
        yield 0, s, s + 3 * odd
    for s in range(3):
        yield 1, s, s + 6 * (1 - odd)


def x_cells(mixed, scale, send_ref):
    table = halves(x_inverse(scale))
    for tile in range(2):
        cells = dot(table, mixed[tile])
        for g in range(GX):
            send_ref[g * 16 + tile * 8 : g * 16 + tile * 8 + 8, :] = cells[g * 8 : g * 8 + 8, :]


def weight_row(pair, c):
    return pl.ds(pair * (KX * C) + c, KX, stride=C)


def packed_row(part, c, tile):
    at = ((part * C + c) * 2 + tile) * 16
    return slice(at, at + 16)


def prepare(odd_ref, weight_ref, fields_ref, cotangent_ref, map_ref, packed_ref, direct_ref, cotangent_t_ref, stage_ref):
    pack_weights(odd_ref, weight_ref, packed_ref)
    stage_ref[...] = jnp.zeros_like(stage_ref)
    for x, y, at in cell_rows():
        stage_ref[at : at + C, :] = dot(map_ref[...], load_cells(fields_ref, x, y))
    direct_ref[...] = stage_ref[...].T
    for x, y, at in cell_rows():
        stage_ref[at : at + C, :] = load_cells(cotangent_ref, x, y)
    cotangent_t_ref[...] = stage_ref[...].T


def pack_weights(odd_ref, weight_ref, packed_ref):
    odd = odd_ref[0]
    packed_ref[...] = jnp.zeros_like(packed_ref)
    for tile, s, pair in slots(odd):
        for part in range(2):
            for c in range(C):
                at = packed_row(part, c, tile).start
                packed_ref[at : at + KX, 20 * s : 20 * s + C] = weight_ref[weight_row(9 * part + pair, c), :]


def group_start():
    lane = lanes(16)
    return jnp.right_shift(lane * 205, 12) * 20


def pick(a, index):
    return jnp.take_along_axis(a, index, axis=1, mode="promise_in_bounds")


def x_mix(recv_ref, packed_ref, send_ref, spec_ref):
    spectrum = x_spectrum(recv_ref, 1.0)
    start = group_start()
    mixed = []
    for tile in range(2):
        spec_ref[tile * 32 : tile * 32 + 32, :] = spectrum[tile]
        real, imag = spectrum[tile][:16], spectrum[tile][16:]
        out_real = jnp.zeros((16, 128), F32)
        out_imag = jnp.zeros((16, 128), F32)
        for c in range(C):
            index = jnp.minimum(start + c, 127)
            sr, si = pick(real, index), pick(imag, index)
            wr = packed_ref[packed_row(0, c, tile), :]
            wi = packed_ref[packed_row(1, c, tile), :]
            out_real = out_real + (sr * wr - si * wi)
            out_imag = out_imag + (sr * wi + si * wr)
        mixed.append(jnp.concatenate([out_real, out_imag], axis=0))
    x_cells(mixed, INV_CELLS, send_ref)


def x_unmix(recv_ref, spec_ref, packed_ref, share_ref, send_ref, high_ref, low_ref):
    share_ref[:64, :] = spec_ref[...]
    spectrum = x_spectrum(recv_ref, INV_CELLS)
    for tile in range(2):
        share_ref[64 + tile * 32 : 96 + tile * 32, :] = spectrum[tile]
        dr, di = spectrum[tile][:16], spectrum[tile][16:]
        for c in range(C):
            wr = packed_ref[packed_row(0, c, tile), :]
            wi = packed_ref[packed_row(1, c, tile), :]
            for part, term in enumerate((dr * wr + di * wi, di * wr - dr * wi)):
                high, low = halves(term)
                at = c * 64 + (tile * 2 + part) * 16
                high_ref[at : at + 16, :] = high
                low_ref[at : at + 16, :] = low
    row, col = row_col(128, 128)
    first = jnp.right_shift(row * 205, 12) * 20
    sums = ((col == first) & (row < 120)).astype(F32).astype(jnp.bfloat16)
    found = jnp.dot(high_ref[...], sums, preferred_element_type=F32) + jnp.dot(
        low_ref[...], sums, preferred_element_type=F32
    )
    back = found[:64]
    for c in range(1, C):
        back = back + pltpu.roll(found[c * 64 : c * 64 + 64], c, axis=1)
    x_cells([back[:32], back[32:]], 1.0, send_ref)


def weight_grad(odd_ref, share_refs, grad_ref):
    odd = odd_ref[0]
    start = group_start()
    owned = list(slots(odd))
    for tile in range(2):
        spec, dual = [], []
        for share_ref in share_refs:
            at = tile * 32
            spec.append([share_ref[at + p * 16 : at + p * 16 + 16, :] for p in range(2)])
            dual.append([share_ref[at + 64 + p * 16 : at + 80 + p * 16, :] for p in range(2)])
        for c in range(C):
            index = jnp.minimum(start + c, 127)
            real = jnp.zeros((16, 128), F32)
            imag = jnp.zeros((16, 128), F32)
            for (er, ei), (dr, di) in zip(spec, dual):
                sr, si = pick(er, index), pick(ei, index)
                real = real + (sr * dr + si * di)
                imag = imag + (sr * di - si * dr)
            for where, s, pair in owned:
                if where == tile:
                    grad_ref[weight_row(pair, c), :] = real[:KX, 20 * s : 20 * s + C]
                    grad_ref[weight_row(9 + pair, c), :] = imag[:KX, 20 * s : 20 * s + C]


def side(odd_ref, map_ref, signal_ref, value_ref, *refs):
    share_refs, (out_ref, direct_ref, grad_ref, stage_ref) = refs[:-4], refs[-4:]
    stage_ref[...] = value_ref[...].T
    for x, y, at in cell_rows():
        store_cells(out_ref, x, y, stage_ref[at : at + C, :])
    stage_ref[...] = signal_ref[...].T
    mapping = halves(map_ref[...])
    for _, _, at in cell_rows():
        direct_ref[at : at + C, :] = dot(mapping, stage_ref[at : at + C, :])
        direct_ref[at + C : at + 32, :] = jnp.zeros((32 - C, NR), F32)
    weight_grad(odd_ref, share_refs, grad_ref)


def activate(recv_ref, turned_ref, table_ref, direct_ref, cotangent_ref, value_ref, signal_ref, send_ref, modes_ref):
    high, low = halves(gather_depth(recv_ref, modes_ref))
    both = jnp.concatenate([high, high], axis=0)
    value_ref[...] = (
        jnp.dot(turned_ref[...], both, preferred_element_type=F32)
        + jnp.dot(turned_ref[:, :192], low, preferred_element_type=F32)
        + direct_ref[...]
    )
    k = math.sqrt(2.0 / math.pi)
    for at in range(0, NR, 64):
        cut = slice(at, at + 64)
        v = value_ref[cut, :]
        square = v * v
        th = jnp.tanh(k * (v + 0.044715 * (square * v)))
        half = 0.5 * (1.0 + th)
        value_ref[cut, :] = v * half
        slope = half + 0.5 * v * (1.0 - th * th) * (k * (1.0 + 3 * 0.044715 * square))
        signal_ref[cut, :] = slope * cotangent_ref[cut, :]
    emit_depth(dot(pair(table_ref), signal_ref[...]), send_ref)


def finish(recv_ref, table_ref, direct_ref, out_ref, modes_ref):
    modes = halves(gather_depth(recv_ref, modes_ref))
    spectral = dot(modes, pair(table_ref), ((0,), (0,)))
    for x, y, at in cell_rows():
        store_cells(out_ref, x, y, spectral[at : at + C, :] + direct_ref[at : at + C, :])


def as_rows(a):
    return a.reshape(C * NX, NY, 4, 128).transpose(0, 2, 1, 3).reshape(640, 128)


def from_rows(a):
    return a.reshape(C * NX, 4, NY, 128).transpose(0, 2, 1, 3).reshape(1, C, NX, NY, NR)


CELLS = (256, NR)
TURNED = (NR, 256)
ROWS = (640, 128)
SEND_Y = (GY * 16, 128)
SEND_X = (GX * 16, 128)
PACKED = (2 * C * 2 * 16, 128)
SHARE = (128, 128)
BF16 = jnp.bfloat16
DMA = pltpu.SemaphoreType.DMA


def stages():
    base = z_table()
    tz, tz_turned = split_table(base, 0), split_table(base.T.copy(), 1)
    modes = [VMEM((192, 256), F32)]
    return dict(
        depth_forward=lambda f: call(
            depth_forward,
            [SEND_Y],
            *(f, tz),
            scratch=[VMEM(ROWS, F32), VMEM(tz.shape, BF16), VMEM(CELLS, F32), DMA((2,))],
            hbm=(0, 1),
            vmem=66_353_664,
        ),
        prepare=lambda o, w, f, ct, b: call(
            prepare, [PACKED, TURNED, TURNED], o, w, f, ct, b, scratch=[VMEM(CELLS, F32)], smem=(0,)
        ),
        y_spectrum=lambda r: call(y_spectrum, [SEND_X], r),
        y_cells=lambda r: call(y_cells, [SEND_Y], r, scratch=[VMEM((24, 512), F32)]),
        x_mix=lambda r, w: call(x_mix, [SEND_X, (64, 128)], r, w),
        x_unmix=lambda r, s, w: call(x_unmix, [SHARE, SEND_X], *(r, s, w), scratch=[VMEM((64 * C, 128), BF16)] * 2),
        side=lambda o, b, sig, val, *shares: call(
            side, [ROWS, CELLS, (2 * 9 * KX * C, C)], *(o, b, sig, val, *shares), scratch=[VMEM(CELLS, F32)], smem=(0,)
        ),
        activate=lambda r, d, ct: call(activate, [TURNED, TURNED, SEND_Y], r, tz_turned, tz, d, ct, scratch=modes),
        finish=lambda r, d: call(finish, [ROWS], r, tz, d, scratch=modes),
    )


def swap(a, axis, n):
    rows = a.shape[0] // n
    return lax.all_to_all(
        a.reshape(n, rows, 128), axis, split_axis=0, concat_axis=0, tiled=True
    ).reshape(n * rows, 128)


def on_device(fields, cotangent, spectral, bypass):
    samples = lax.axis_size("dp")
    st = stages()
    odd = (lax.axis_index("gx") & 1).astype(jnp.int32).reshape(1)
    rows = as_rows(fields)
    weights = spectral.reshape(2 * 9 * KX * C, C)
    to_y = functools.partial(swap, axis="gy", n=GY)
    to_x = functools.partial(swap, axis="gx", n=GX)
    sent = st["y_spectrum"](to_y(st["depth_forward"](rows)))
    packed, direct, turned = st["prepare"](odd, weights, rows, as_rows(cotangent), bypass.T)
    mixed, spec = st["x_mix"](to_x(sent), packed)
    arrived = to_y(st["y_cells"](to_x(mixed)))
    value, signal, sent = st["activate"](arrived, direct, turned)
    share, sent = st["x_unmix"](to_x(st["y_spectrum"](to_y(sent))), spec, packed)
    arrived = to_x(sent)
    shares = [share]
    for step in range(1, samples):
        shares.append(lax.ppermute(share, "dp", [(i, (i + step) % samples) for i in range(samples)]))
    arrived, *shares = lax.optimization_barrier((arrived, *shares))
    output, direct, grad = st["side"](odd, bypass, signal, value, *shares)
    field_grad = st["finish"](to_y(st["y_cells"](arrived)), direct)
    return (from_rows(output), from_rows(field_grad), grad.reshape(spectral.shape))


def solution(mesh):
    cells = P("dp", None, "gx", "gy", None)
    modes = P(None, "gx", "gy", None, None, None)
    return jax.shard_map(
        on_device,
        mesh=mesh,
        in_specs=(cells, cells, modes, P()),
        out_specs=(cells, cells, modes),
        check_vma=False,
    )
```

```python
import functools
import math

import jax
import jax.numpy as jnp
import numpy as np
from jax import lax
from jax.experimental import pallas as pl
from jax.experimental.pallas import tpu as pltpu
from jax.sharding import PartitionSpec as P


C = 20
NX, NY, NR = 4, 2, 512
GX, GY = 8, 16
S6 = 6
KX = 12
F32 = jnp.float32
VMEM = pltpu.VMEM
INV_CELLS = 1.0 / (32 * 32 * 512)
INTERPRET = False


def freq(i, n):
    return i if i < n // 2 else i - n


def z_table():
    r = np.arange(NR)
    z, t = r // 8, r % 8
    out = np.zeros((S6, 2, GY, NR))
    for s in range(S6):
        for j in range(GY):
            m = 6 * j + s
            kz, kt = freq(m // 8, 12), freq(m % 8, 8)
            w = (kz * z * 8 + kt * t * 64) % 512
            ang = w * (2.0 * math.pi / 512)
            out[s, 0, j] = np.cos(ang)
            out[s, 1, j] = -np.sin(ang)
    return out.reshape(S6 * 2 * GY, NR).astype(np.float32)


def split_table(table, axis):
    high = table.astype(jnp.bfloat16)
    low = (table - high.astype(np.float32)).astype(jnp.bfloat16)
    return np.concatenate([high, low], axis=axis)


COS = [(-1) ** i * math.pi ** (2 * i) / math.factorial(2 * i) for i in range(11)]
SIN = [(-1) ** i * math.pi ** (2 * i + 1) / math.factorial(2 * i + 1) for i in range(11)]


def rotation(mode, cell, part_out, part_in, sign, scale):
    k = jnp.where(mode >= 6, mode - 12, mode)
    turns = (((k * cell + 16) & 31) - 16).astype(F32) * (1.0 / 16)
    u = turns * turns
    cos = jnp.full_like(u, COS[-1])
    sin = jnp.full_like(u, SIN[-1])
    for i in range(len(COS) - 2, -1, -1):
        cos = cos * u + COS[i]
        sin = sin * u + SIN[i]
    sin = sin * turns * sign
    value = jnp.where(part_out == part_in, cos, jnp.where(part_out == 1, sin, -sin))
    return value * scale if scale != 1.0 else value


def row_col(rows, cols):
    shape = (rows, cols)
    return lax.broadcasted_iota(jnp.int32, shape, 0), lax.broadcasted_iota(jnp.int32, shape, 1)


def y_forward():
    row, col = row_col(48, 64)
    part = (row >= 24).astype(jnp.int32)
    rest = row - 24 * part
    mode = 3 * (rest & 7) + (rest >> 3)
    return rotation(mode, 2 * (col & 15) + (col >> 5), part, (col >> 4) & 1, -1.0, 1.0)


def y_inverse():
    row, col = row_col(64, 24)
    part = (col >= 12).astype(jnp.int32)
    rest = col - 12 * part
    mode = 3 * (rest & 3) + (rest >> 2)
    return rotation(mode, 2 * (row & 15) + (row >> 5), (row >> 4) & 1, part, 1.0, 1.0)


def x_forward(scale):
    row, col = row_col(32, 64)
    return rotation(row & 15, col >> 1, row >> 4, col & 1, -1.0, scale)


def x_inverse(scale):
    row, col = row_col(64, 32)
    return rotation(col & 15, row >> 1, row & 1, col >> 4, 1.0, scale)


def call(body, outs, *args, scratch=(), smem=(), hbm=(), vmem=16 << 20, flops=10**7):
    specs = [
        pl.BlockSpec(memory_space=pltpu.SMEM if i in smem else pltpu.HBM if i in hbm else VMEM)
        for i in range(len(args))
    ]
    shapes = [jax.ShapeDtypeStruct(s, F32) for s in outs]
    nbytes = 4 * sum(math.prod(s) for s in outs) + sum(a.size * a.dtype.itemsize for a in args)
    got = pl.pallas_call(
        body,
        out_shape=shapes,
        in_specs=specs,
        out_specs=[pl.BlockSpec(memory_space=VMEM)] * len(outs),
        scratch_shapes=list(scratch),
        compiler_params=pltpu.CompilerParams(vmem_limit_bytes=vmem),
        cost_estimate=pl.CostEstimate(flops=flops, bytes_accessed=nbytes, transcendentals=0),
        interpret=INTERPRET,
    )(*args)
    return got if len(outs) > 1 else got[0]


def halves(a):
    high = a.astype(jnp.bfloat16)
    return high, (a - high.astype(F32)).astype(jnp.bfloat16)


def dot(a, b, dims=((1,), (0,))):
    ah, al = a if isinstance(a, tuple) else halves(a)
    bh, bl = b if isinstance(b, tuple) else halves(b)

    def one(x, y):
        return lax.dot_general(x, y, (dims, ((), ())), preferred_element_type=F32)

    return one(ah, bh) + (one(ah, bl) + one(al, bh))


def pair(ref):
    rows = ref.shape[0] // 2
    return ref[:rows, :], ref[rows:, :]


def lanes(rows):
    return lax.broadcasted_iota(jnp.int32, (rows, 128), 1)


def load_cells(ref, x, y):
    return jnp.concatenate(
        [ref[pl.ds(x * 8 + tile * 2 + y, C, stride=32), :] for tile in range(4)], axis=1
    )


def store_cells(ref, x, y, value):
    for tile in range(4):
        ref[pl.ds(x * 8 + tile * 2 + y, C, stride=32), :] = value[:, tile * 128 : tile * 128 + 128]


def emit_depth(modes, send_ref):
    lane = lanes(GY)
    for y in range(NY):
        for x in range(NX):
            for part in range(2):
                total = jnp.zeros((GY, 128), F32)
                for s in range(S6):
                    at = (s * 2 + part) * GY
                    piece = modes[at : at + GY, y * 128 : y * 128 + 128]
                    shift = (20 * s - 32 * x) % 128
                    if shift:
                        piece = pltpu.roll(piece, shift, axis=1)
                    total = jnp.where((lane >= 20 * s) & (lane < 20 * s + 20), piece, total)
                send_ref[pl.ds(x * 4 + y * 2 + part, GY, stride=16), :] = total


def gather_depth(recv_ref, modes_ref):
    lane = lanes(GY)
    for y in range(NY):
        for part in range(2):
            pieces = [recv_ref[pl.ds(x * 4 + y * 2 + part, GY, stride=16), :] for x in range(NX)]
            for s in range(S6):
                total = jnp.zeros((GY, 128), F32)
                for x in range(NX):
                    shift = (32 * x - 20 * s) % 128
                    piece = pltpu.roll(pieces[x], shift, axis=1) if shift else pieces[x]
                    total = jnp.where((lane >= 32 * x) & (lane < 32 * x + 20), piece, total)
                at = (s * 2 + part) * GY
                modes_ref[at : at + GY, y * 128 : y * 128 + 128] = total
    return modes_ref[...]


def cell_rows():
    for y in range(NY):
        for x in range(NX):
            yield x, y, (y * NX + x) * 32


def depth_forward(fields_hbm, table_hbm, send_ref, fields_ref, table_ref, stage_ref, sems):
    fields_copy = pltpu.make_async_copy(fields_hbm, fields_ref, sems.at[0])
    table_copy = pltpu.make_async_copy(table_hbm, table_ref, sems.at[1])
    fields_copy.start()
    table_copy.start()
    stage_ref[...] = jnp.zeros_like(stage_ref)
    fields_copy.wait()
    for x, y, at in cell_rows():
        stage_ref[at : at + C, :] = load_cells(fields_ref, x, y)
    table_copy.wait()
    emit_depth(dot(pair(table_ref), stage_ref[...], ((1,), (1,))), send_ref)


def y_spectrum(recv_ref, send_ref):
    columns = []
    for x in range(NX):
        columns.append(
            jnp.concatenate(
                [recv_ref[pl.ds(x * 4 + row, GY, stride=16), :] for row in range(4)], axis=0
            )
        )
    turned = dot(y_forward(), jnp.concatenate(columns, axis=1))
    for x in range(NX):
        for part in range(2):
            row = x * 2 + part
            t0, t1, t2 = [
                turned[part * 24 + t * 8 : part * 24 + t * 8 + 8, x * 128 : x * 128 + 128] for t in range(3)
            ]
            send_ref[pl.ds(row, 4, stride=32), :] = t0[:4]
            send_ref[pl.ds(8 + row, 4, stride=32), :] = t1[:4]
            send_ref[pl.ds(16 + row, 4, stride=32), :] = t2[:4]
            send_ref[pl.ds(24 + row, 4, stride=32), :] = pltpu.roll(t1, 68, axis=1)[:4]


def y_cells(recv_ref, send_ref, stage_ref):
    lane = lanes(4)
    for x in range(NX):
        for part in range(2):
            row = x * 2 + part
            t0, low, t2, high = [recv_ref[pl.ds(slot * 8 + row, 4, stride=32), :] for slot in range(4)]
            at = part * 12
            cut = slice(x * 128, x * 128 + 128)
            stage_ref[at : at + 4, cut] = t0
            stage_ref[at + 4 : at + 8, cut] = jnp.where(lane < 60, low, pltpu.roll(high, 60, axis=1))
            stage_ref[at + 8 : at + 12, cut] = t2
    cells = dot(y_inverse(), stage_ref[...])
    for x in range(NX):
        for row in range(4):
            send_ref[pl.ds(x * 4 + row, GY, stride=16), :] = cells[
                row * 16 : row * 16 + 16, x * 128 : x * 128 + 128
            ]


def x_spectrum(recv_ref, scale):
    found = []
    table = halves(x_forward(scale))
    for tile in range(2):
        data = jnp.concatenate(
            [recv_ref[src * 16 + tile * 8 : src * 16 + tile * 8 + 8, :] for src in range(GX)], axis=0
        )
        found.append(dot(table, data))
    return found


def slots(odd):
    for s in range(6):
        yield 0, s, s + 3 * odd
    for s in range(3):
        yield 1, s, s + 6 * (1 - odd)


def x_cells(mixed, scale, send_ref):
    table = halves(x_inverse(scale))
    for tile in range(2):
        cells = dot(table, mixed[tile])
        for g in range(GX):
            send_ref[g * 16 + tile * 8 : g * 16 + tile * 8 + 8, :] = cells[g * 8 : g * 8 + 8, :]


def weight_row(pair, c):
    return pl.ds(pair * (KX * C) + c, KX, stride=C)


def packed_row(part, c, tile):
    at = ((part * C + c) * 2 + tile) * 16
    return slice(at, at + 16)


def prepare(odd_ref, weight_ref, fields_ref, cotangent_ref, map_ref, packed_ref, direct_ref, cotangent_t_ref, stage_ref):
    pack_weights(odd_ref, weight_ref, packed_ref)
    mapping = halves(map_ref[...])
    stage_ref[...] = jnp.zeros_like(stage_ref)
    for x, y, at in cell_rows():
        stage_ref[at : at + C, :] = dot(mapping, load_cells(fields_ref, x, y), ((0,), (0,)))
    direct_ref[...] = stage_ref[...].T
    for x, y, at in cell_rows():
        stage_ref[at : at + C, :] = load_cells(cotangent_ref, x, y)
    cotangent_t_ref[...] = stage_ref[...].T


def pack_weights(odd_ref, weight_ref, packed_ref):
    odd = odd_ref[0]
    packed_ref[...] = jnp.zeros_like(packed_ref)
    for tile, s, pair in slots(odd):
        for part in range(2):
            for c in range(C):
                at = packed_row(part, c, tile).start
                packed_ref[at : at + KX, 20 * s : 20 * s + C] = weight_ref[weight_row(9 * part + pair, c), :]


def group_start():
    lane = lanes(16)
    return jnp.right_shift(lane * 205, 12) * 20


def pick(a, index):
    return jnp.take_along_axis(a, index, axis=1, mode="promise_in_bounds")


def x_mix(recv_ref, packed_ref, send_ref, spec_ref):
    spectrum = x_spectrum(recv_ref, 1.0)
    start = group_start()
    mixed = []
    for tile in range(2):
        spec_ref[tile * 32 : tile * 32 + 32, :] = spectrum[tile]
        real, imag = spectrum[tile][:16], spectrum[tile][16:]
        out_real = jnp.zeros((16, 128), F32)
        out_imag = jnp.zeros((16, 128), F32)
        for c in range(C):
            index = jnp.minimum(start + c, 127)
            sr, si = pick(real, index), pick(imag, index)
            wr = packed_ref[packed_row(0, c, tile), :]
            wi = packed_ref[packed_row(1, c, tile), :]
            out_real = out_real + (sr * wr - si * wi)
            out_imag = out_imag + (sr * wi + si * wr)
        mixed.append(jnp.concatenate([out_real, out_imag], axis=0))
    x_cells(mixed, INV_CELLS, send_ref)


def x_unmix(recv_ref, spec_ref, packed_ref, share_ref, send_ref, high_ref, low_ref):
    share_ref[:64, :] = spec_ref[...]
    spectrum = x_spectrum(recv_ref, INV_CELLS)
    for tile in range(2):
        share_ref[64 + tile * 32 : 96 + tile * 32, :] = spectrum[tile]
        dr, di = spectrum[tile][:16], spectrum[tile][16:]
        for c in range(C):
            wr = packed_ref[packed_row(0, c, tile), :]
            wi = packed_ref[packed_row(1, c, tile), :]
            for part, term in enumerate((dr * wr + di * wi, di * wr - dr * wi)):
                high, low = halves(term)
                at = c * 64 + (tile * 2 + part) * 16
                high_ref[at : at + 16, :] = high
                low_ref[at : at + 16, :] = low
    row, col = row_col(128, 128)
    first = jnp.right_shift(row * 205, 12) * 20
    sums = ((col == first) & (row < 120)).astype(F32).astype(jnp.bfloat16)
    found = jnp.dot(high_ref[...], sums, preferred_element_type=F32) + jnp.dot(
        low_ref[...], sums, preferred_element_type=F32
    )
    back = found[:64]
    for c in range(1, C):
        back = back + pltpu.roll(found[c * 64 : c * 64 + 64], c, axis=1)
    x_cells([back[:32], back[32:]], 1.0, send_ref)


def weight_grad(odd_ref, share_refs, grad_ref):
    odd = odd_ref[0]
    start = group_start()
    owned = list(slots(odd))
    for tile in range(2):
        spec, dual = [], []
        for share_ref in share_refs:
            at = tile * 32
            spec.append([share_ref[at + p * 16 : at + p * 16 + 16, :] for p in range(2)])
            dual.append([share_ref[at + 64 + p * 16 : at + 80 + p * 16, :] for p in range(2)])
        for c in range(C):
            index = jnp.minimum(start + c, 127)
            real = jnp.zeros((16, 128), F32)
            imag = jnp.zeros((16, 128), F32)
            for (er, ei), (dr, di) in zip(spec, dual):
                sr, si = pick(er, index), pick(ei, index)
                real = real + (sr * dr + si * di)
                imag = imag + (sr * di - si * dr)
            for where, s, pair in owned:
                if where == tile:
                    grad_ref[weight_row(pair, c), :] = real[:KX, 20 * s : 20 * s + C]
                    grad_ref[weight_row(9 + pair, c), :] = imag[:KX, 20 * s : 20 * s + C]


def side(odd_ref, map_ref, signal_ref, value_ref, *refs):
    share_refs, (out_ref, direct_ref, grad_ref, stage_ref) = refs[:-4], refs[-4:]
    stage_ref[...] = value_ref[...].T
    for x, y, at in cell_rows():
        store_cells(out_ref, x, y, stage_ref[at : at + C, :])
    stage_ref[...] = signal_ref[...].T
    mapping = halves(map_ref[...])
    for _, _, at in cell_rows():
        direct_ref[at : at + C, :] = dot(mapping, stage_ref[at : at + C, :])
        direct_ref[at + C : at + 32, :] = jnp.zeros((32 - C, NR), F32)
    weight_grad(odd_ref, share_refs, grad_ref)


def activate(recv_ref, turned_ref, table_ref, direct_ref, cotangent_ref, value_ref, signal_ref, send_ref, modes_ref):
    high, low = halves(gather_depth(recv_ref, modes_ref))
    both = jnp.concatenate([high, high], axis=0)
    value_ref[...] = (
        jnp.dot(turned_ref[...], both, preferred_element_type=F32)
        + jnp.dot(turned_ref[:, :192], low, preferred_element_type=F32)
        + direct_ref[...]
    )
    k = math.sqrt(2.0 / math.pi)
    for at in range(0, NR, 64):
        cut = slice(at, at + 64)
        v = value_ref[cut, :]
        square = v * v
        th = jnp.tanh(k * (v + 0.044715 * (square * v)))
        half = 0.5 * (1.0 + th)
        value_ref[cut, :] = v * half
        slope = half + 0.5 * v * (1.0 - th * th) * (k * (1.0 + 3 * 0.044715 * square))
        signal_ref[cut, :] = slope * cotangent_ref[cut, :]
    emit_depth(dot(pair(table_ref), signal_ref[...]), send_ref)


def finish(recv_ref, table_ref, direct_ref, out_ref, modes_ref):
    modes = halves(gather_depth(recv_ref, modes_ref))
    spectral = dot(modes, pair(table_ref), ((0,), (0,)))
    for x, y, at in cell_rows():
        store_cells(out_ref, x, y, spectral[at : at + C, :] + direct_ref[at : at + C, :])


def as_rows(a):
    return a.reshape(C * NX, NY, 4, 128).transpose(0, 2, 1, 3).reshape(640, 128)


def from_rows(a):
    return a.reshape(C * NX, 4, NY, 128).transpose(0, 2, 1, 3).reshape(1, C, NX, NY, NR)


CELLS = (256, NR)
TURNED = (NR, 256)
ROWS = (640, 128)
SEND_Y = (GY * 16, 128)
SEND_X = (GX * 16, 128)
PACKED = (2 * C * 2 * 16, 128)
SHARE = (128, 128)
BF16 = jnp.bfloat16
DMA = pltpu.SemaphoreType.DMA


def stages():
    base = z_table()
    tz, tz_turned = split_table(base, 0), split_table(base.T.copy(), 1)
    modes = [VMEM((192, 256), F32)]
    return dict(
        depth_forward=lambda f: call(
            depth_forward,
            [SEND_Y],
            *(f, tz),
            scratch=[VMEM(ROWS, F32), VMEM(tz.shape, BF16), VMEM(CELLS, F32), DMA((2,))],
            hbm=(0, 1),
            vmem=66_313_216,
        ),
        prepare=lambda o, w, f, ct, b: call(
            prepare, [PACKED, TURNED, TURNED], o, w, f, ct, b, scratch=[VMEM(CELLS, F32)], smem=(0,)
        ),
        y_spectrum=lambda r: call(y_spectrum, [SEND_X], r),
        y_cells=lambda r: call(y_cells, [SEND_Y], r, scratch=[VMEM((24, 512), F32)]),
        x_mix=lambda r, w: call(x_mix, [SEND_X, (64, 128)], r, w),
        x_unmix=lambda r, s, w: call(x_unmix, [SHARE, SEND_X], *(r, s, w), scratch=[VMEM((64 * C, 128), BF16)] * 2),
        side=lambda o, b, sig, val, *shares: call(
            side, [ROWS, CELLS, (2 * 9 * KX * C, C)], *(o, b, sig, val, *shares), scratch=[VMEM(CELLS, F32)], smem=(0,)
        ),
        activate=lambda r, d, ct: call(activate, [TURNED, TURNED, SEND_Y], r, tz_turned, tz, d, ct, scratch=modes),
        finish=lambda r, d: call(finish, [ROWS], r, tz, d, scratch=modes),
    )


def swap(a, axis, n):
    rows = a.shape[0] // n
    return lax.all_to_all(
        a.reshape(n, rows, 128), axis, split_axis=0, concat_axis=0, tiled=True
    ).reshape(n * rows, 128)


def on_device(fields, cotangent, spectral, bypass):
    samples = lax.axis_size("dp")
    st = stages()
    odd = (lax.axis_index("gx") & 1).astype(jnp.int32).reshape(1)
    rows = as_rows(fields)
    weights = spectral.reshape(2 * 9 * KX * C, C)
    to_y = functools.partial(swap, axis="gy", n=GY)
    to_x = functools.partial(swap, axis="gx", n=GX)
    arrived = to_y(st["depth_forward"](rows))
    packed, direct, turned = st["prepare"](odd, weights, rows, as_rows(cotangent), bypass)
    sent = st["y_spectrum"](arrived)
    mixed, spec = st["x_mix"](to_x(sent), packed)
    arrived = to_y(st["y_cells"](to_x(mixed)))
    value, signal, sent = st["activate"](arrived, direct, turned)
    share, sent = st["x_unmix"](to_x(st["y_spectrum"](to_y(sent))), spec, packed)
    arrived = to_x(sent)
    sent = st["y_cells"](arrived)
    shares = [share]
    for step in range(1, samples):
        shares.append(lax.ppermute(share, "dp", [(i, (i + step) % samples) for i in range(samples)]))
    output, direct, grad = st["side"](odd, bypass, signal, value, *shares)
    field_grad = st["finish"](to_y(sent), direct)
    return (from_rows(output), from_rows(field_grad), grad.reshape(spectral.shape))


def solution(mesh):
    cells = P("dp", None, "gx", "gy", None)
    modes = P(None, "gx", "gy", None, None, None)
    return jax.shard_map(
        on_device,
        mesh=mesh,
        in_specs=(cells, cells, modes, P()),
        out_specs=(cells, cells, modes),
        check_vma=False,
    )
```

```python
import functools
import math

import jax
import jax.numpy as jnp
import numpy as np
from jax import lax
from jax.experimental import pallas as pl
from jax.experimental.pallas import tpu as pltpu
from jax.sharding import PartitionSpec as P


C = 20
NX, NY, NR = 4, 2, 512
GX, GY = 8, 16
S6 = 6
KX = 12
F32 = jnp.float32
VMEM = pltpu.VMEM
INV_CELLS = 1.0 / (32 * 32 * 512)
INTERPRET = False


def freq(i, n):
    return i if i < n // 2 else i - n


def z_table():
    r = np.arange(NR)
    z, t = r // 8, r % 8
    out = np.zeros((S6, 2, GY, NR))
    for s in range(S6):
        for j in range(GY):
            m = 6 * j + s
            kz, kt = freq(m // 8, 12), freq(m % 8, 8)
            w = (kz * z * 8 + kt * t * 64) % 512
            ang = w * (2.0 * math.pi / 512)
            out[s, 0, j] = np.cos(ang)
            out[s, 1, j] = -np.sin(ang)
    return out.reshape(S6 * 2 * GY, NR).astype(np.float32)


def split_table(table, axis):
    high = table.astype(jnp.bfloat16)
    low = (table - high.astype(np.float32)).astype(jnp.bfloat16)
    return np.concatenate([high, low], axis=axis)


COS = [(-1) ** i * math.pi ** (2 * i) / math.factorial(2 * i) for i in range(11)]
SIN = [(-1) ** i * math.pi ** (2 * i + 1) / math.factorial(2 * i + 1) for i in range(11)]


def rotation(mode, cell, part_out, part_in, sign, scale):
    k = jnp.where(mode >= 6, mode - 12, mode)
    turns = (((k * cell + 16) & 31) - 16).astype(F32) * (1.0 / 16)
    u = turns * turns
    cos = jnp.full_like(u, COS[-1])
    sin = jnp.full_like(u, SIN[-1])
    for i in range(len(COS) - 2, -1, -1):
        cos = cos * u + COS[i]
        sin = sin * u + SIN[i]
    sin = sin * turns * sign
    value = jnp.where(part_out == part_in, cos, jnp.where(part_out == 1, sin, -sin))
    return value * scale if scale != 1.0 else value


def row_col(rows, cols):
    shape = (rows, cols)
    return lax.broadcasted_iota(jnp.int32, shape, 0), lax.broadcasted_iota(jnp.int32, shape, 1)


def y_forward():
    row, col = row_col(48, 64)
    part = (row >= 24).astype(jnp.int32)
    rest = row - 24 * part
    mode = 3 * (rest & 7) + (rest >> 3)
    return rotation(mode, 2 * (col & 15) + (col >> 5), part, (col >> 4) & 1, -1.0, 1.0)


def y_inverse():
    row, col = row_col(64, 24)
    part = (col >= 12).astype(jnp.int32)
    rest = col - 12 * part
    mode = 3 * (rest & 3) + (rest >> 2)
    return rotation(mode, 2 * (row & 15) + (row >> 5), (row >> 4) & 1, part, 1.0, 1.0)


def x_forward(scale):
    row, col = row_col(32, 64)
    return rotation(row & 15, col >> 1, row >> 4, col & 1, -1.0, scale)


def x_inverse(scale):
    row, col = row_col(64, 32)
    return rotation(col & 15, row >> 1, row & 1, col >> 4, 1.0, scale)


def call(body, outs, *args, scratch=(), smem=(), hbm=(), vmem=16 << 20, flops=10**7):
    specs = [
        pl.BlockSpec(memory_space=pltpu.SMEM if i in smem else pltpu.HBM if i in hbm else VMEM)
        for i in range(len(args))
    ]
    shapes = [jax.ShapeDtypeStruct(s, F32) for s in outs]
    nbytes = 4 * sum(math.prod(s) for s in outs) + sum(a.size * a.dtype.itemsize for a in args)
    got = pl.pallas_call(
        body,
        out_shape=shapes,
        in_specs=specs,
        out_specs=[pl.BlockSpec(memory_space=VMEM)] * len(outs),
        scratch_shapes=list(scratch),
        compiler_params=pltpu.CompilerParams(vmem_limit_bytes=vmem),
        cost_estimate=pl.CostEstimate(flops=flops, bytes_accessed=nbytes, transcendentals=0),
        interpret=INTERPRET,
    )(*args)
    return got if len(outs) > 1 else got[0]


def halves(a):
    high = a.astype(jnp.bfloat16)
    return high, (a - high.astype(F32)).astype(jnp.bfloat16)


def dot(a, b, dims=((1,), (0,))):
    ah, al = a if isinstance(a, tuple) else halves(a)
    bh, bl = b if isinstance(b, tuple) else halves(b)

    def one(x, y):
        return lax.dot_general(x, y, (dims, ((), ())), preferred_element_type=F32)

    return one(ah, bh) + (one(ah, bl) + one(al, bh))


def pair(ref):
    rows = ref.shape[0] // 2
    return ref[:rows, :], ref[rows:, :]


def lanes(rows):
    return lax.broadcasted_iota(jnp.int32, (rows, 128), 1)


def load_cells(ref, x, y):
    return jnp.concatenate(
        [ref[pl.ds(x * 8 + tile * 2 + y, C, stride=32), :] for tile in range(4)], axis=1
    )


def store_cells(ref, x, y, value):
    for tile in range(4):
        ref[pl.ds(x * 8 + tile * 2 + y, C, stride=32), :] = value[:, tile * 128 : tile * 128 + 128]


def emit_depth(modes, send_ref):
    lane = lanes(GY)
    for y in range(NY):
        for x in range(NX):
            for part in range(2):
                total = jnp.zeros((GY, 128), F32)
                for s in range(S6):
                    at = (s * 2 + part) * GY
                    piece = modes[at : at + GY, y * 128 : y * 128 + 128]
                    shift = (20 * s - 32 * x) % 128
                    if shift:
                        piece = pltpu.roll(piece, shift, axis=1)
                    total = jnp.where((lane >= 20 * s) & (lane < 20 * s + 20), piece, total)
                send_ref[pl.ds(x * 4 + y * 2 + part, GY, stride=16), :] = total


def gather_depth(recv_ref, modes_ref):
    lane = lanes(GY)
    for y in range(NY):
        for part in range(2):
            pieces = [recv_ref[pl.ds(x * 4 + y * 2 + part, GY, stride=16), :] for x in range(NX)]
            for s in range(S6):
                total = jnp.zeros((GY, 128), F32)
                for x in range(NX):
                    shift = (32 * x - 20 * s) % 128
                    piece = pltpu.roll(pieces[x], shift, axis=1) if shift else pieces[x]
                    total = jnp.where((lane >= 32 * x) & (lane < 32 * x + 20), piece, total)
                at = (s * 2 + part) * GY
                modes_ref[at : at + GY, y * 128 : y * 128 + 128] = total
    return modes_ref[...]


def cell_rows():
    for y in range(NY):
        for x in range(NX):
            yield x, y, (y * NX + x) * 32


def depth_forward(fields_hbm, table_hbm, send_ref, fields_ref, table_ref, stage_ref, sems):
    fields_copy = pltpu.make_async_copy(fields_hbm, fields_ref, sems.at[0])
    table_copy = pltpu.make_async_copy(table_hbm, table_ref, sems.at[1])
    fields_copy.start()
    table_copy.start()
    stage_ref[...] = jnp.zeros_like(stage_ref)
    fields_copy.wait()
    for x, y, at in cell_rows():
        stage_ref[at : at + C, :] = load_cells(fields_ref, x, y)
    table_copy.wait()
    emit_depth(dot(pair(table_ref), stage_ref[...], ((1,), (1,))), send_ref)


def y_spectrum(recv_ref, send_ref):
    columns = []
    for x in range(NX):
        columns.append(
            jnp.concatenate(
                [recv_ref[pl.ds(x * 4 + row, GY, stride=16), :] for row in range(4)], axis=0
            )
        )
    turned = dot(y_forward(), jnp.concatenate(columns, axis=1))
    for x in range(NX):
        for part in range(2):
            row = x * 2 + part
            t0, t1, t2 = [
                turned[part * 24 + t * 8 : part * 24 + t * 8 + 8, x * 128 : x * 128 + 128] for t in range(3)
            ]
            send_ref[pl.ds(row, 4, stride=32), :] = t0[:4]
            send_ref[pl.ds(8 + row, 4, stride=32), :] = t1[:4]
            send_ref[pl.ds(16 + row, 4, stride=32), :] = t2[:4]
            send_ref[pl.ds(24 + row, 4, stride=32), :] = pltpu.roll(t1, 68, axis=1)[:4]


def y_cells(recv_ref, send_ref, stage_ref):
    lane = lanes(4)
    for x in range(NX):
        for part in range(2):
            row = x * 2 + part
            t0, low, t2, high = [recv_ref[pl.ds(slot * 8 + row, 4, stride=32), :] for slot in range(4)]
            at = part * 12
            cut = slice(x * 128, x * 128 + 128)
            stage_ref[at : at + 4, cut] = t0
            stage_ref[at + 4 : at + 8, cut] = jnp.where(lane < 60, low, pltpu.roll(high, 60, axis=1))
            stage_ref[at + 8 : at + 12, cut] = t2
    cells = dot(y_inverse(), stage_ref[...])
    for x in range(NX):
        for row in range(4):
            send_ref[pl.ds(x * 4 + row, GY, stride=16), :] = cells[
                row * 16 : row * 16 + 16, x * 128 : x * 128 + 128
            ]


def x_spectrum(recv_ref, scale):
    found = []
    table = halves(x_forward(scale))
    for tile in range(2):
        data = jnp.concatenate(
            [recv_ref[src * 16 + tile * 8 : src * 16 + tile * 8 + 8, :] for src in range(GX)], axis=0
        )
        found.append(dot(table, data))
    return found


def slots(odd):
    for s in range(6):
        yield 0, s, s + 3 * odd
    for s in range(3):
        yield 1, s, s + 6 * (1 - odd)


def x_cells(mixed, scale, send_ref):
    table = halves(x_inverse(scale))
    for tile in range(2):
        cells = dot(table, mixed[tile])
        for g in range(GX):
            send_ref[g * 16 + tile * 8 : g * 16 + tile * 8 + 8, :] = cells[g * 8 : g * 8 + 8, :]


def weight_row(pair, c):
    return pl.ds(pair * (KX * C) + c, KX, stride=C)


def packed_row(part, c, tile):
    at = ((part * C + c) * 2 + tile) * 16
    return slice(at, at + 16)


def prepare(odd_ref, weight_ref, fields_ref, cotangent_ref, map_ref, packed_ref, direct_ref, cotangent_t_ref, stage_ref):
    pack_weights(odd_ref, weight_ref, packed_ref)
    mapping = halves(map_ref[...])
    stage_ref[...] = jnp.zeros_like(stage_ref)
    for x, y, at in cell_rows():
        stage_ref[at : at + C, :] = dot(mapping, load_cells(fields_ref, x, y), ((0,), (0,)))
    direct_ref[...] = stage_ref[...].T
    for x, y, at in cell_rows():
        stage_ref[at : at + C, :] = load_cells(cotangent_ref, x, y)
    cotangent_t_ref[...] = stage_ref[...].T


def pack_weights(odd_ref, weight_ref, packed_ref):
    odd = odd_ref[0]
    packed_ref[...] = jnp.zeros_like(packed_ref)
    for tile, s, pair in slots(odd):
        for part in range(2):
            for c in range(C):
                at = packed_row(part, c, tile).start
                packed_ref[at : at + KX, 20 * s : 20 * s + C] = weight_ref[weight_row(9 * part + pair, c), :]


def group_start():
    lane = lanes(16)
    return jnp.right_shift(lane * 205, 12) * 20


def pick(a, index):
    return jnp.take_along_axis(a, index, axis=1, mode="promise_in_bounds")


def x_mix(recv_ref, packed_ref, send_ref, spec_ref):
    spectrum = x_spectrum(recv_ref, 1.0)
    start = group_start()
    mixed = []
    for tile in range(2):
        spec_ref[tile * 32 : tile * 32 + 32, :] = spectrum[tile]
        real, imag = spectrum[tile][:16], spectrum[tile][16:]
        out_real = jnp.zeros((16, 128), F32)
        out_imag = jnp.zeros((16, 128), F32)
        for c in range(C):
            index = jnp.minimum(start + c, 127)
            sr, si = pick(real, index), pick(imag, index)
            wr = packed_ref[packed_row(0, c, tile), :]
            wi = packed_ref[packed_row(1, c, tile), :]
            out_real = out_real + (sr * wr - si * wi)
            out_imag = out_imag + (sr * wi + si * wr)
        mixed.append(jnp.concatenate([out_real, out_imag], axis=0))
    x_cells(mixed, INV_CELLS, send_ref)


def x_unmix(recv_ref, spec_ref, packed_ref, share_ref, send_ref, high_ref, low_ref):
    share_ref[:64, :] = spec_ref[...]
    spectrum = x_spectrum(recv_ref, INV_CELLS)
    for tile in range(2):
        share_ref[64 + tile * 32 : 96 + tile * 32, :] = spectrum[tile]
        dr, di = spectrum[tile][:16], spectrum[tile][16:]
        for c in range(C):
            wr = packed_ref[packed_row(0, c, tile), :]
            wi = packed_ref[packed_row(1, c, tile), :]
            for part, term in enumerate((dr * wr + di * wi, di * wr - dr * wi)):
                high, low = halves(term)
                at = c * 64 + (tile * 2 + part) * 16
                high_ref[at : at + 16, :] = high
                low_ref[at : at + 16, :] = low
    row, col = row_col(128, 128)
    first = jnp.right_shift(row * 205, 12) * 20
    sums = ((col == first) & (row < 120)).astype(F32).astype(jnp.bfloat16)
    found = jnp.dot(high_ref[...], sums, preferred_element_type=F32) + jnp.dot(
        low_ref[...], sums, preferred_element_type=F32
    )
    back = found[:64]
    for c in range(1, C):
        back = back + pltpu.roll(found[c * 64 : c * 64 + 64], c, axis=1)
    x_cells([back[:32], back[32:]], 1.0, send_ref)


def weight_grad(odd_ref, near_ref, far_ref, grad_ref):
    odd = odd_ref[0]
    start = group_start()
    owned = list(slots(odd))
    for tile in range(2):
        spec, dual = [], []
        for share_ref in (near_ref, far_ref):
            for at in (tile * 32, 128 + tile * 32):
                spec.append([share_ref[at + p * 16 : at + p * 16 + 16, :] for p in range(2)])
                dual.append([share_ref[at + 64 + p * 16 : at + 80 + p * 16, :] for p in range(2)])
        for c in range(C):
            index = jnp.minimum(start + c, 127)
            real = jnp.zeros((16, 128), F32)
            imag = jnp.zeros((16, 128), F32)
            for (er, ei), (dr, di) in zip(spec, dual):
                sr, si = pick(er, index), pick(ei, index)
                real = real + (sr * dr + si * di)
                imag = imag + (sr * di - si * dr)
            for where, s, pair in owned:
                if where == tile:
                    grad_ref[weight_row(pair, c), :] = real[:KX, 20 * s : 20 * s + C]
                    grad_ref[weight_row(9 + pair, c), :] = imag[:KX, 20 * s : 20 * s + C]


def join(mine_ref, other_ref, out_ref):
    out_ref[:128, :] = mine_ref[...]
    out_ref[128:, :] = other_ref[...]


def emit(map_ref, signal_ref, value_ref, out_ref, direct_ref, stage_ref):
    stage_ref[...] = value_ref[...].T
    for x, y, at in cell_rows():
        store_cells(out_ref, x, y, stage_ref[at : at + C, :])
    stage_ref[...] = signal_ref[...].T
    mapping = halves(map_ref[...])
    for _, _, at in cell_rows():
        direct_ref[at : at + C, :] = dot(mapping, stage_ref[at : at + C, :])
        direct_ref[at + C : at + 32, :] = jnp.zeros((32 - C, NR), F32)


def activate(recv_ref, turned_ref, table_ref, direct_ref, cotangent_ref, value_ref, signal_ref, send_ref, modes_ref):
    high, low = halves(gather_depth(recv_ref, modes_ref))
    both = jnp.concatenate([high, high], axis=0)
    value_ref[...] = (
        jnp.dot(turned_ref[...], both, preferred_element_type=F32)
        + jnp.dot(turned_ref[:, :192], low, preferred_element_type=F32)
        + direct_ref[...]
    )
    k = math.sqrt(2.0 / math.pi)
    for at in range(0, NR, 64):
        cut = slice(at, at + 64)
        v = value_ref[cut, :]
        square = v * v
        th = jnp.tanh(k * (v + 0.044715 * (square * v)))
        half = 0.5 * (1.0 + th)
        value_ref[cut, :] = v * half
        slope = half + 0.5 * v * (1.0 - th * th) * (k * (1.0 + 3 * 0.044715 * square))
        signal_ref[cut, :] = slope * cotangent_ref[cut, :]
    emit_depth(dot(pair(table_ref), signal_ref[...]), send_ref)


def finish(recv_ref, table_ref, direct_ref, out_ref, modes_ref):
    modes = halves(gather_depth(recv_ref, modes_ref))
    spectral = dot(modes, pair(table_ref), ((0,), (0,)))
    for x, y, at in cell_rows():
        store_cells(out_ref, x, y, spectral[at : at + C, :] + direct_ref[at : at + C, :])


def as_rows(a):
    return a.reshape(C * NX, NY, 4, 128).transpose(0, 2, 1, 3).reshape(640, 128)


def from_rows(a):
    return a.reshape(C * NX, 4, NY, 128).transpose(0, 2, 1, 3).reshape(1, C, NX, NY, NR)


CELLS = (256, NR)
TURNED = (NR, 256)
ROWS = (640, 128)
SEND_Y = (GY * 16, 128)
SEND_X = (GX * 16, 128)
PACKED = (2 * C * 2 * 16, 128)
SHARE = (128, 128)
BF16 = jnp.bfloat16
DMA = pltpu.SemaphoreType.DMA


def stages():
    base = z_table()
    tz, tz_turned = split_table(base, 0), split_table(base.T.copy(), 1)
    modes = [VMEM((192, 256), F32)]
    return dict(
        depth_forward=lambda f: call(
            depth_forward,
            [SEND_Y],
            *(f, tz),
            scratch=[VMEM(ROWS, F32), VMEM(tz.shape, BF16), VMEM(CELLS, F32), DMA((2,))],
            hbm=(0, 1),
            vmem=66_313_216,
        ),
        prepare=lambda o, w, f, ct, b: call(
            prepare, [PACKED, TURNED, TURNED], o, w, f, ct, b, scratch=[VMEM(CELLS, F32)], smem=(0,)
        ),
        y_spectrum=lambda r: call(y_spectrum, [SEND_X], r),
        y_cells=lambda r: call(y_cells, [SEND_Y], r, scratch=[VMEM((24, 512), F32)]),
        x_mix=lambda r, w: call(x_mix, [SEND_X, (64, 128)], r, w),
        x_unmix=lambda r, s, w: call(x_unmix, [SHARE, SEND_X], *(r, s, w), scratch=[VMEM((64 * C, 128), BF16)] * 2),
        join=lambda a, b: call(join, [(256, 128)], a, b),
        emit=lambda b, sig, val: call(emit, [ROWS, CELLS], b, sig, val, scratch=[VMEM(CELLS, F32)]),
        weight_grad=lambda o, near, far: call(weight_grad, [(2 * 9 * KX * C, C)], o, near, far, smem=(0,)),
        activate=lambda r, d, ct: call(activate, [TURNED, TURNED, SEND_Y], r, tz_turned, tz, d, ct, scratch=modes),
        finish=lambda r, d: call(finish, [ROWS], r, tz, d, scratch=modes),
    )


def swap(a, axis, n):
    rows = a.shape[0] // n
    return lax.all_to_all(
        a.reshape(n, rows, 128), axis, split_axis=0, concat_axis=0, tiled=True
    ).reshape(n * rows, 128)


def on_device(fields, cotangent, spectral, bypass):
    assert lax.axis_size("dp") == 4
    st = stages()
    odd = (lax.axis_index("gx") & 1).astype(jnp.int32).reshape(1)
    rows = as_rows(fields)
    weights = spectral.reshape(2 * 9 * KX * C, C)
    to_y = functools.partial(swap, axis="gy", n=GY)
    to_x = functools.partial(swap, axis="gx", n=GX)
    arrived = to_y(st["depth_forward"](rows))
    packed, direct, turned = st["prepare"](odd, weights, rows, as_rows(cotangent), bypass)
    sent = st["y_spectrum"](arrived)
    mixed, spec = st["x_mix"](to_x(sent), packed)
    arrived = to_y(st["y_cells"](to_x(mixed)))
    value, signal, sent = st["activate"](arrived, direct, turned)
    share, sent = st["x_unmix"](to_x(st["y_spectrum"](to_y(sent))), spec, packed)
    arrived = to_x(sent)
    sent = st["y_cells"](arrived)
    other = lax.ppermute(share, "dp", [(i, i ^ 1) for i in range(4)])
    joined = st["join"](share, other)
    rest = lax.ppermute(joined, "dp", [(i, 3 - i) for i in range(4)])
    output, direct = st["emit"](bypass, signal, value)
    grad = st["weight_grad"](odd, joined, rest)
    field_grad = st["finish"](to_y(sent), direct)
    return (from_rows(output), from_rows(field_grad), grad.reshape(spectral.shape))


def solution(mesh):
    cells = P("dp", None, "gx", "gy", None)
    modes = P(None, "gx", "gy", None, None, None)
    return jax.shard_map(
        on_device,
        mesh=mesh,
        in_specs=(cells, cells, modes, P()),
        out_specs=(cells, cells, modes),
        check_vma=False,
    )
```

```python
import functools
import math

import jax
import jax.numpy as jnp
import numpy as np
from jax import lax
from jax.experimental import pallas as pl
from jax.experimental.pallas import tpu as pltpu
from jax.sharding import PartitionSpec as P


C = 20
NX, NY, NR = 4, 2, 512
GX, GY = 8, 16
S6 = 6
KX = 12
SHARE_ROWS = 6 * KX
F32 = jnp.float32
VMEM = pltpu.VMEM
INV_CELLS = 1.0 / (32 * 32 * 512)
INTERPRET = False


def freq(i, n):
    return i if i < n // 2 else i - n


def z_table():
    r = np.arange(NR)
    z, t = r // 8, r % 8
    out = np.zeros((S6, 2, GY, NR))
    for s in range(S6):
        for j in range(GY):
            m = 6 * j + s
            kz, kt = freq(m // 8, 12), freq(m % 8, 8)
            w = (kz * z * 8 + kt * t * 64) % 512
            ang = w * (2.0 * math.pi / 512)
            out[s, 0, j] = np.cos(ang)
            out[s, 1, j] = -np.sin(ang)
    return out.reshape(S6 * 2 * GY, NR).astype(np.float32)


def split_table(table, axis):
    high = table.astype(jnp.bfloat16)
    low = (table - high.astype(np.float32)).astype(jnp.bfloat16)
    return np.concatenate([high, low], axis=axis)


COS = [(-1) ** i * math.pi ** (2 * i) / math.factorial(2 * i) for i in range(11)]
SIN = [(-1) ** i * math.pi ** (2 * i + 1) / math.factorial(2 * i + 1) for i in range(11)]


def rotation(mode, cell, part_out, part_in, sign, scale):
    k = jnp.where(mode >= 6, mode - 12, mode)
    turns = (((k * cell + 16) & 31) - 16).astype(F32) * (1.0 / 16)
    u = turns * turns
    cos = jnp.full_like(u, COS[-1])
    sin = jnp.full_like(u, SIN[-1])
    for i in range(len(COS) - 2, -1, -1):
        cos = cos * u + COS[i]
        sin = sin * u + SIN[i]
    sin = sin * turns * sign
    value = jnp.where(part_out == part_in, cos, jnp.where(part_out == 1, sin, -sin))
    return value * scale if scale != 1.0 else value


def row_col(rows, cols):
    shape = (rows, cols)
    return lax.broadcasted_iota(jnp.int32, shape, 0), lax.broadcasted_iota(jnp.int32, shape, 1)


def y_forward():
    row, col = row_col(48, 64)
    part = (row >= 24).astype(jnp.int32)
    rest = row - 24 * part
    mode = 3 * (rest & 7) + (rest >> 3)
    return rotation(mode, 2 * (col & 15) + (col >> 5), part, (col >> 4) & 1, -1.0, 1.0)


def y_inverse():
    row, col = row_col(64, 24)
    part = (col >= 12).astype(jnp.int32)
    rest = col - 12 * part
    mode = 3 * (rest & 3) + (rest >> 2)
    return rotation(mode, 2 * (row & 15) + (row >> 5), (row >> 4) & 1, part, 1.0, 1.0)


def x_forward(scale):
    row, col = row_col(32, 64)
    return rotation(row & 15, col >> 1, row >> 4, col & 1, -1.0, scale)


def x_inverse(scale):
    row, col = row_col(64, 32)
    return rotation(col & 15, row >> 1, row & 1, col >> 4, 1.0, scale)


def call(body, outs, *args, scratch=(), smem=(), hbm=(), hbm_out=False, vmem=16 << 20, flops=10**7):
    specs = [
        pl.BlockSpec(memory_space=pltpu.SMEM if i in smem else pltpu.HBM if i in hbm else VMEM)
        for i in range(len(args))
    ]
    shapes = [jax.ShapeDtypeStruct(s, F32) for s in outs]
    nbytes = 4 * sum(math.prod(s) for s in outs) + sum(a.size * a.dtype.itemsize for a in args)
    got = pl.pallas_call(
        body,
        out_shape=shapes,
        in_specs=specs,
        out_specs=[pl.BlockSpec(memory_space=pl.ANY if hbm_out else VMEM)] * len(outs),
        scratch_shapes=list(scratch),
        compiler_params=pltpu.CompilerParams(vmem_limit_bytes=vmem),
        cost_estimate=pl.CostEstimate(flops=flops, bytes_accessed=nbytes, transcendentals=0),
        interpret=INTERPRET,
    )(*args)
    return got if len(outs) > 1 else got[0]


def halves(a):
    high = a.astype(jnp.bfloat16)
    return high, (a - high.astype(F32)).astype(jnp.bfloat16)


def dot(a, b, dims=((1,), (0,))):
    ah, al = a if isinstance(a, tuple) else halves(a)
    bh, bl = b if isinstance(b, tuple) else halves(b)

    def one(x, y):
        return lax.dot_general(x, y, (dims, ((), ())), preferred_element_type=F32)

    return one(ah, bh) + (one(ah, bl) + one(al, bh))


def pair(ref):
    rows = ref.shape[0] // 2
    return ref[:rows, :], ref[rows:, :]


def lanes(rows):
    return lax.broadcasted_iota(jnp.int32, (rows, 128), 1)


def load_cells(ref, x, y):
    return jnp.concatenate(
        [ref[pl.ds(x * 8 + tile * 2 + y, C, stride=32), :] for tile in range(4)], axis=1
    )


def store_cells(ref, x, y, value):
    for tile in range(4):
        ref[pl.ds(x * 8 + tile * 2 + y, C, stride=32), :] = value[:, tile * 128 : tile * 128 + 128]


def emit_depth(modes, send_ref):
    lane = lanes(GY)
    for y in range(NY):
        for x in range(NX):
            for part in range(2):
                total = jnp.zeros((GY, 128), F32)
                for s in range(S6):
                    at = (s * 2 + part) * GY
                    piece = modes[at : at + GY, y * 128 : y * 128 + 128]
                    shift = (20 * s - 32 * x) % 128
                    if shift:
                        piece = pltpu.roll(piece, shift, axis=1)
                    total = jnp.where((lane >= 20 * s) & (lane < 20 * s + 20), piece, total)
                send_ref[pl.ds(x * 4 + y * 2 + part, GY, stride=16), :] = total


def gather_depth(recv_ref, modes_ref):
    lane = lanes(GY)
    for y in range(NY):
        for part in range(2):
            pieces = [recv_ref[pl.ds(x * 4 + y * 2 + part, GY, stride=16), :] for x in range(NX)]
            for s in range(S6):
                total = jnp.zeros((GY, 128), F32)
                for x in range(NX):
                    shift = (32 * x - 20 * s) % 128
                    piece = pltpu.roll(pieces[x], shift, axis=1) if shift else pieces[x]
                    total = jnp.where((lane >= 32 * x) & (lane < 32 * x + 20), piece, total)
                at = (s * 2 + part) * GY
                modes_ref[at : at + GY, y * 128 : y * 128 + 128] = total
    return modes_ref[...]


def cell_rows():
    for y in range(NY):
        for x in range(NX):
            yield x, y, (y * NX + x) * 32


def depth_forward(fields_hbm, table_hbm, send_ref, fields_ref, table_ref, stage_ref, sems):
    fields_copy = pltpu.make_async_copy(fields_hbm, fields_ref, sems.at[0])
    table_copy = pltpu.make_async_copy(table_hbm, table_ref, sems.at[1])
    fields_copy.start()
    table_copy.start()
    stage_ref[...] = jnp.zeros_like(stage_ref)
    fields_copy.wait()
    for x, y, at in cell_rows():
        stage_ref[at : at + C, :] = load_cells(fields_ref, x, y)
    table_copy.wait()
    emit_depth(dot(pair(table_ref), stage_ref[...], ((1,), (1,))), send_ref)


def y_spectrum(recv_ref, send_ref):
    columns = []
    for x in range(NX):
        columns.append(
            jnp.concatenate(
                [recv_ref[pl.ds(x * 4 + row, GY, stride=16), :] for row in range(4)], axis=0
            )
        )
    turned = dot(y_forward(), jnp.concatenate(columns, axis=1))
    for x in range(NX):
        for part in range(2):
            row = x * 2 + part
            t0, t1, t2 = [
                turned[part * 24 + t * 8 : part * 24 + t * 8 + 8, x * 128 : x * 128 + 128] for t in range(3)
            ]
            send_ref[pl.ds(row, 4, stride=32), :] = t0[:4]
            send_ref[pl.ds(8 + row, 4, stride=32), :] = t1[:4]
            send_ref[pl.ds(16 + row, 4, stride=32), :] = t2[:4]
            send_ref[pl.ds(24 + row, 4, stride=32), :] = pltpu.roll(t1, 68, axis=1)[:4]


def y_cells(recv_ref, send_ref, stage_ref):
    lane = lanes(4)
    for x in range(NX):
        for part in range(2):
            row = x * 2 + part
            t0, low, t2, high = [recv_ref[pl.ds(slot * 8 + row, 4, stride=32), :] for slot in range(4)]
            at = part * 12
            cut = slice(x * 128, x * 128 + 128)
            stage_ref[at : at + 4, cut] = t0
            stage_ref[at + 4 : at + 8, cut] = jnp.where(lane < 60, low, pltpu.roll(high, 60, axis=1))
            stage_ref[at + 8 : at + 12, cut] = t2
    cells = dot(y_inverse(), stage_ref[...])
    for x in range(NX):
        for row in range(4):
            send_ref[pl.ds(x * 4 + row, GY, stride=16), :] = cells[
                row * 16 : row * 16 + 16, x * 128 : x * 128 + 128
            ]


def x_spectrum(recv_ref, scale):
    found = []
    table = halves(x_forward(scale))
    for tile in range(2):
        data = jnp.concatenate(
            [recv_ref[src * 16 + tile * 8 : src * 16 + tile * 8 + 8, :] for src in range(GX)], axis=0
        )
        found.append(dot(table, data))
    return found


def slots(odd):
    for s in range(6):
        yield 0, s, s + 3 * odd
    for s in range(3):
        yield 1, s, s + 6 * (1 - odd)


def x_cells(mixed, scale, send_ref):
    table = halves(x_inverse(scale))
    for tile in range(2):
        cells = dot(table, mixed[tile])
        for g in range(GX):
            send_ref[g * 16 + tile * 8 : g * 16 + tile * 8 + 8, :] = cells[g * 8 : g * 8 + 8, :]


def weight_row(pair, c):
    return pl.ds(pair * (KX * C) + c, KX, stride=C)


def packed_row(part, c, tile):
    at = ((part * C + c) * 2 + tile) * 16
    return slice(at, at + 16)


def prepare(odd_ref, weight_ref, fields_ref, cotangent_ref, map_ref, packed_ref, direct_ref, cotangent_t_ref, stage_ref):
    pack_weights(odd_ref, weight_ref, packed_ref)
    mapping = halves(map_ref[...])
    stage_ref[...] = jnp.zeros_like(stage_ref)
    for x, y, at in cell_rows():
        stage_ref[at : at + C, :] = dot(mapping, load_cells(fields_ref, x, y), ((0,), (0,)))
    direct_ref[...] = stage_ref[...].T
    for x, y, at in cell_rows():
        stage_ref[at : at + C, :] = load_cells(cotangent_ref, x, y)
    cotangent_t_ref[...] = stage_ref[...].T


def pack_weights(odd_ref, weight_ref, packed_ref):
    odd = odd_ref[0]
    packed_ref[...] = jnp.zeros_like(packed_ref)
    for tile, s, pair in slots(odd):
        for part in range(2):
            for c in range(C):
                at = packed_row(part, c, tile).start
                packed_ref[at : at + KX, 20 * s : 20 * s + C] = weight_ref[weight_row(9 * part + pair, c), :]


def group_start():
    lane = lanes(16)
    return jnp.right_shift(lane * 205, 12) * 20


def pick(a, index):
    return jnp.take_along_axis(a, index, axis=1, mode="promise_in_bounds")


def x_mix(recv_ref, packed_ref, send_ref, spec_ref):
    spectrum = x_spectrum(recv_ref, 1.0)
    start = group_start()
    mixed = []
    for tile in range(2):
        spec_ref[tile * 32 : tile * 32 + 32, :] = spectrum[tile]
        real, imag = spectrum[tile][:16], spectrum[tile][16:]
        out_real = jnp.zeros((16, 128), F32)
        out_imag = jnp.zeros((16, 128), F32)
        for c in range(C):
            index = jnp.minimum(start + c, 127)
            sr, si = pick(real, index), pick(imag, index)
            wr = packed_ref[packed_row(0, c, tile), :]
            wi = packed_ref[packed_row(1, c, tile), :]
            out_real = out_real + (sr * wr - si * wi)
            out_imag = out_imag + (sr * wi + si * wr)
        mixed.append(jnp.concatenate([out_real, out_imag], axis=0))
    x_cells(mixed, INV_CELLS, send_ref)


def x_unmix(recv_ref, spec_ref, packed_ref, share_ref, send_ref, high_ref, low_ref):
    spectrum = x_spectrum(recv_ref, INV_CELLS)
    lane = lanes(KX)
    for part in range(2):
        low, high = part * 16, part * KX
        share_ref[high : high + KX, :] = spec_ref[low : low + KX, :]
        share_ref[24 + high : 24 + high + KX, :] = spectrum[0][low : low + KX]
        dual = pltpu.roll(spectrum[1][low : low + 16], 60, axis=1)[:KX]
        share_ref[48 + high : 48 + high + KX, :] = jnp.where(lane < 60, spec_ref[32 + low : 32 + low + KX, :], dual)
    for tile in range(2):
        dr, di = spectrum[tile][:16], spectrum[tile][16:]
        for c in range(C):
            wr = packed_ref[packed_row(0, c, tile), :]
            wi = packed_ref[packed_row(1, c, tile), :]
            for part, term in enumerate((dr * wr + di * wi, di * wr - dr * wi)):
                high, low = halves(term)
                at = c * 64 + (tile * 2 + part) * 16
                high_ref[at : at + 16, :] = high
                low_ref[at : at + 16, :] = low
    row, col = row_col(128, 128)
    first = jnp.right_shift(row * 205, 12) * 20
    sums = ((col == first) & (row < 120)).astype(F32).astype(jnp.bfloat16)
    found = jnp.dot(high_ref[...], sums, preferred_element_type=F32) + jnp.dot(
        low_ref[...], sums, preferred_element_type=F32
    )
    back = found[:64]
    for c in range(1, C):
        back = back + pltpu.roll(found[c * 64 : c * 64 + 64], c, axis=1)
    x_cells([back[:32], back[32:]], 1.0, send_ref)


def weight_grad(odd_ref, near_ref, far_ref, grad_hbm, *scratch):
    odd = odd_ref[0]
    buffers, sems = scratch[:2], scratch[2]
    start = group_start()[:KX]
    copies = []
    for tile in range(2):
        buffer, pairs = buffers[tile], (6, 3)[tile]
        samples = []
        for share_ref in (near_ref, far_ref):
            for at in (0, SHARE_ROWS):
                parts = [share_ref[at + k * KX : at + k * KX + KX, :] for k in range(6)]
                if tile == 0:
                    samples.append(parts[:4])
                else:
                    samples.append(parts[4:] + [pltpu.roll(a, 68, axis=1) for a in parts[4:]])
        rows = pairs * KX * C
        for c in range(C):
            index = jnp.minimum(start + c, 127)
            real = jnp.zeros((KX, 128), F32)
            imag = jnp.zeros((KX, 128), F32)
            for er, ei, dr, di in samples:
                sr, si = pick(er, index), pick(ei, index)
                real = real + (sr * dr + si * di)
                imag = imag + (sr * di - si * dr)
            for s in range(pairs):
                buffer[weight_row(s, c), :] = real[:, 20 * s : 20 * s + C]
                buffer[pl.ds(rows + s * (KX * C) + c, KX, stride=C), :] = imag[:, 20 * s : 20 * s + C]
        first = (3 * odd if tile == 0 else 6 * (1 - odd)) * (KX * C)
        for part in range(2):
            copy = pltpu.make_async_copy(
                buffer.at[pl.ds(part * rows, rows), :],
                grad_hbm.at[pl.ds(pl.multiple_of(part * (9 * KX * C) + first, 8), rows), :],
                sems.at[tile * 2 + part],
            )
            copy.start()
            copies.append(copy)
    for copy in copies:
        copy.wait()


def join(mine_ref, other_ref, out_ref):
    out_ref[:SHARE_ROWS, :] = mine_ref[...]
    out_ref[SHARE_ROWS:, :] = other_ref[...]


def emit(map_ref, signal_ref, value_ref, out_ref, direct_ref, stage_ref):
    stage_ref[...] = value_ref[...].T
    for x, y, at in cell_rows():
        store_cells(out_ref, x, y, stage_ref[at : at + C, :])
    stage_ref[...] = signal_ref[...].T
    mapping = halves(map_ref[...])
    for _, _, at in cell_rows():
        direct_ref[at : at + C, :] = dot(mapping, stage_ref[at : at + C, :])
        direct_ref[at + C : at + 32, :] = jnp.zeros((32 - C, NR), F32)


def activate(recv_ref, turned_ref, table_ref, direct_ref, cotangent_ref, value_ref, signal_ref, send_ref, modes_ref):
    high, low = halves(gather_depth(recv_ref, modes_ref))
    both = jnp.concatenate([high, high], axis=0)
    value_ref[...] = (
        jnp.dot(turned_ref[...], both, preferred_element_type=F32)
        + jnp.dot(turned_ref[:, :192], low, preferred_element_type=F32)
        + direct_ref[...]
    )
    k = math.sqrt(2.0 / math.pi)
    for at in range(0, NR, 64):
        cut = slice(at, at + 64)
        v = value_ref[cut, :]
        square = v * v
        th = jnp.tanh(k * (v + 0.044715 * (square * v)))
        half = 0.5 * (1.0 + th)
        value_ref[cut, :] = v * half
        slope = half + 0.5 * v * (1.0 - th * th) * (k * (1.0 + 3 * 0.044715 * square))
        signal_ref[cut, :] = slope * cotangent_ref[cut, :]
    emit_depth(dot(pair(table_ref), signal_ref[...]), send_ref)


def finish(recv_ref, table_ref, direct_ref, out_ref, modes_ref):
    modes = halves(gather_depth(recv_ref, modes_ref))
    spectral = dot(modes, pair(table_ref), ((0,), (0,)))
    for x, y, at in cell_rows():
        store_cells(out_ref, x, y, spectral[at : at + C, :] + direct_ref[at : at + C, :])


def as_rows(a):
    return a.reshape(C * NX, NY, 4, 128).transpose(0, 2, 1, 3).reshape(640, 128)


def from_rows(a):
    return a.reshape(C * NX, 4, NY, 128).transpose(0, 2, 1, 3).reshape(1, C, NX, NY, NR)


CELLS = (256, NR)
TURNED = (NR, 256)
ROWS = (640, 128)
SEND_Y = (GY * 16, 128)
SEND_X = (GX * 16, 128)
PACKED = (2 * C * 2 * 16, 128)
SHARE = (SHARE_ROWS, 128)
BF16 = jnp.bfloat16
DMA = pltpu.SemaphoreType.DMA


def stages():
    base = z_table()
    tz, tz_turned = split_table(base, 0), split_table(base.T.copy(), 1)
    modes = [VMEM((192, 256), F32)]
    return dict(
        depth_forward=lambda f: call(
            depth_forward,
            [SEND_Y],
            *(f, tz),
            scratch=[VMEM(ROWS, F32), VMEM(tz.shape, BF16), VMEM(CELLS, F32), DMA((2,))],
            hbm=(0, 1),
            vmem=66_313_216,
        ),
        prepare=lambda o, w, f, ct, b: call(
            prepare, [PACKED, TURNED, TURNED], o, w, f, ct, b, scratch=[VMEM(CELLS, F32)], smem=(0,)
        ),
        y_spectrum=lambda r: call(y_spectrum, [SEND_X], r),
        y_cells=lambda r: call(y_cells, [SEND_Y], r, scratch=[VMEM((24, 512), F32)]),
        x_mix=lambda r, w: call(x_mix, [SEND_X, (64, 128)], r, w),
        x_unmix=lambda r, s, w: call(x_unmix, [SHARE, SEND_X], *(r, s, w), scratch=[VMEM((64 * C, 128), BF16)] * 2),
        join=lambda a, b: call(join, [(2 * SHARE_ROWS, 128)], a, b),
        emit=lambda b, sig, val: call(emit, [ROWS, CELLS], b, sig, val, scratch=[VMEM(CELLS, F32)]),
        weight_grad=lambda o, near, far: call(
            weight_grad,
            [(2 * 9 * KX * C, C)],
            *(o, near, far),
            scratch=[VMEM((2 * 6 * KX * C, C), F32), VMEM((2 * 3 * KX * C, C), F32), DMA((4,))],
            smem=(0,),
            hbm_out=True,
        ),
        activate=lambda r, d, ct: call(activate, [TURNED, TURNED, SEND_Y], r, tz_turned, tz, d, ct, scratch=modes),
        finish=lambda r, d: call(finish, [ROWS], r, tz, d, scratch=modes),
    )


def swap(a, axis, n):
    rows = a.shape[0] // n
    return lax.all_to_all(
        a.reshape(n, rows, 128), axis, split_axis=0, concat_axis=0, tiled=True
    ).reshape(n * rows, 128)


def on_device(fields, cotangent, spectral, bypass):
    assert lax.axis_size("dp") == 4
    st = stages()
    odd = (lax.axis_index("gx") & 1).astype(jnp.int32).reshape(1)
    rows = as_rows(fields)
    weights = spectral.reshape(2 * 9 * KX * C, C)
    to_y = functools.partial(swap, axis="gy", n=GY)
    to_x = functools.partial(swap, axis="gx", n=GX)
    arrived = to_y(st["depth_forward"](rows))
    packed, direct, turned = st["prepare"](odd, weights, rows, as_rows(cotangent), bypass)
    sent = st["y_spectrum"](arrived)
    mixed, spec = st["x_mix"](to_x(sent), packed)
    arrived = to_y(st["y_cells"](to_x(mixed)))
    value, signal, sent = st["activate"](arrived, direct, turned)
    share, sent = st["x_unmix"](to_x(st["y_spectrum"](to_y(sent))), spec, packed)
    arrived = to_x(sent)
    sent = st["y_cells"](arrived)
    arrived = to_y(sent)
    other = lax.ppermute(share, "dp", [(i, i ^ 1) for i in range(4)])
    joined = st["join"](share, other)
    rest = lax.ppermute(joined, "dp", [(i, 3 - i) for i in range(4)])
    output, direct = st["emit"](bypass, signal, value)
    grad = st["weight_grad"](odd, joined, rest)
    field_grad = st["finish"](arrived, direct)
    return (from_rows(output), from_rows(field_grad), grad.reshape(spectral.shape))


def solution(mesh):
    cells = P("dp", None, "gx", "gy", None)
    modes = P(None, "gx", "gy", None, None, None)
    return jax.shard_map(
        on_device,
        mesh=mesh,
        in_specs=(cells, cells, modes, P()),
        out_specs=(cells, cells, modes),
        check_vma=False,
    )
```

```python
import functools
import math

import jax
import jax.numpy as jnp
import numpy as np
from jax import lax
from jax.experimental import pallas as pl
from jax.experimental.pallas import tpu as pltpu
from jax.sharding import PartitionSpec as P


C = 20
NX, NY, NR = 4, 2, 512
GX, GY = 8, 16
S6 = 6
KX = 12
SHARE_ROWS = 6 * KX
F32 = jnp.float32
VMEM = pltpu.VMEM
INV_CELLS = 1.0 / (32 * 32 * 512)
INTERPRET = False


def freq(i, n):
    return i if i < n // 2 else i - n


def z_table():
    r = np.arange(NR)
    z, t = r // 8, r % 8
    out = np.zeros((S6, 2, GY, NR))
    for s in range(S6):
        for j in range(GY):
            m = 6 * j + s
            kz, kt = freq(m // 8, 12), freq(m % 8, 8)
            w = (kz * z * 8 + kt * t * 64) % 512
            ang = w * (2.0 * math.pi / 512)
            out[s, 0, j] = np.cos(ang)
            out[s, 1, j] = -np.sin(ang)
    return out.reshape(S6 * 2 * GY, NR).astype(np.float32)


def split_table(table, axis):
    high = table.astype(jnp.bfloat16)
    low = (table - high.astype(np.float32)).astype(jnp.bfloat16)
    return np.concatenate([high, low], axis=axis)


COS = [(-1) ** i * math.pi ** (2 * i) / math.factorial(2 * i) for i in range(11)]
SIN = [(-1) ** i * math.pi ** (2 * i + 1) / math.factorial(2 * i + 1) for i in range(11)]


def rotation(mode, cell, part_out, part_in, sign, scale):
    k = jnp.where(mode >= 6, mode - 12, mode)
    turns = (((k * cell + 16) & 31) - 16).astype(F32) * (1.0 / 16)
    u = turns * turns
    cos = jnp.full_like(u, COS[-1])
    sin = jnp.full_like(u, SIN[-1])
    for i in range(len(COS) - 2, -1, -1):
        cos = cos * u + COS[i]
        sin = sin * u + SIN[i]
    sin = sin * turns * sign
    value = jnp.where(part_out == part_in, cos, jnp.where(part_out == 1, sin, -sin))
    return value * scale if scale != 1.0 else value


def row_col(rows, cols):
    shape = (rows, cols)
    return lax.broadcasted_iota(jnp.int32, shape, 0), lax.broadcasted_iota(jnp.int32, shape, 1)


def y_forward():
    row, col = row_col(48, 64)
    part = (row >= 24).astype(jnp.int32)
    rest = row - 24 * part
    mode = 3 * (rest & 7) + (rest >> 3)
    return rotation(mode, 2 * (col & 15) + (col >> 5), part, (col >> 4) & 1, -1.0, 1.0)


def y_inverse():
    row, col = row_col(64, 24)
    part = (col >= 12).astype(jnp.int32)
    rest = col - 12 * part
    mode = 3 * (rest & 3) + (rest >> 2)
    return rotation(mode, 2 * (row & 15) + (row >> 5), (row >> 4) & 1, part, 1.0, 1.0)


def x_forward(scale):
    row, col = row_col(32, 64)
    return rotation(row & 15, col >> 1, row >> 4, col & 1, -1.0, scale)


def x_inverse(scale):
    row, col = row_col(64, 32)
    return rotation(col & 15, row >> 1, row & 1, col >> 4, 1.0, scale)


def call(body, outs, *args, scratch=(), smem=(), hbm=(), hbm_out=False, vmem=16 << 20, flops=10**7):
    specs = [
        pl.BlockSpec(memory_space=pltpu.SMEM if i in smem else pltpu.HBM if i in hbm else VMEM)
        for i in range(len(args))
    ]
    shapes = [jax.ShapeDtypeStruct(s, F32) for s in outs]
    nbytes = 4 * sum(math.prod(s) for s in outs) + sum(a.size * a.dtype.itemsize for a in args)
    got = pl.pallas_call(
        body,
        out_shape=shapes,
        in_specs=specs,
        out_specs=[pl.BlockSpec(memory_space=pl.ANY if hbm_out else VMEM)] * len(outs),
        scratch_shapes=list(scratch),
        compiler_params=pltpu.CompilerParams(vmem_limit_bytes=vmem),
        cost_estimate=pl.CostEstimate(flops=flops, bytes_accessed=nbytes, transcendentals=0),
        interpret=INTERPRET,
    )(*args)
    return got if len(outs) > 1 else got[0]


def halves(a):
    high = a.astype(jnp.bfloat16)
    return high, (a - high.astype(F32)).astype(jnp.bfloat16)


def dot(a, b, dims=((1,), (0,))):
    ah, al = a if isinstance(a, tuple) else halves(a)
    bh, bl = b if isinstance(b, tuple) else halves(b)

    def one(x, y):
        return lax.dot_general(x, y, (dims, ((), ())), preferred_element_type=F32)

    return one(ah, bh) + (one(ah, bl) + one(al, bh))


def pair(ref):
    rows = ref.shape[0] // 2
    return ref[:rows, :], ref[rows:, :]


def lanes(rows):
    return lax.broadcasted_iota(jnp.int32, (rows, 128), 1)


def load_cells(ref, x, y):
    return jnp.concatenate(
        [ref[pl.ds(x * 8 + tile * 2 + y, C, stride=32), :] for tile in range(4)], axis=1
    )


def store_cells(ref, x, y, value):
    for tile in range(4):
        ref[pl.ds(x * 8 + tile * 2 + y, C, stride=32), :] = value[:, tile * 128 : tile * 128 + 128]


def emit_depth(modes, send_ref):
    lane = lanes(GY)
    for y in range(NY):
        for x in range(NX):
            for part in range(2):
                total = jnp.zeros((GY, 128), F32)
                for s in range(S6):
                    at = (s * 2 + part) * GY
                    piece = modes[at : at + GY, y * 128 : y * 128 + 128]
                    shift = (20 * s - 32 * x) % 128
                    if shift:
                        piece = pltpu.roll(piece, shift, axis=1)
                    total = jnp.where((lane >= 20 * s) & (lane < 20 * s + 20), piece, total)
                send_ref[pl.ds(x * 4 + y * 2 + part, GY, stride=16), :] = total


def gather_depth(recv_ref, modes_ref):
    lane = lanes(GY)
    for y in range(NY):
        for part in range(2):
            pieces = [recv_ref[pl.ds(x * 4 + y * 2 + part, GY, stride=16), :] for x in range(NX)]
            for s in range(S6):
                total = jnp.zeros((GY, 128), F32)
                for x in range(NX):
                    shift = (32 * x - 20 * s) % 128
                    piece = pltpu.roll(pieces[x], shift, axis=1) if shift else pieces[x]
                    total = jnp.where((lane >= 32 * x) & (lane < 32 * x + 20), piece, total)
                at = (s * 2 + part) * GY
                modes_ref[at : at + GY, y * 128 : y * 128 + 128] = total
    return modes_ref[...]


def cell_rows():
    for y in range(NY):
        for x in range(NX):
            yield x, y, (y * NX + x) * 32


def depth_forward(fields_hbm, table_hbm, send_ref, fields_ref, table_ref, stage_ref, sems):
    fields_copy = pltpu.make_async_copy(fields_hbm, fields_ref, sems.at[0])
    table_copy = pltpu.make_async_copy(table_hbm, table_ref, sems.at[1])
    fields_copy.start()
    table_copy.start()
    stage_ref[...] = jnp.zeros_like(stage_ref)
    fields_copy.wait()
    for x, y, at in cell_rows():
        stage_ref[at : at + C, :] = load_cells(fields_ref, x, y)
    table_copy.wait()
    emit_depth(dot(pair(table_ref), stage_ref[...], ((1,), (1,))), send_ref)


def y_spectrum(recv_ref, send_ref):
    columns = []
    for x in range(NX):
        columns.append(
            jnp.concatenate(
                [recv_ref[pl.ds(x * 4 + row, GY, stride=16), :] for row in range(4)], axis=0
            )
        )
    turned = dot(y_forward(), jnp.concatenate(columns, axis=1))
    for x in range(NX):
        for part in range(2):
            row = x * 2 + part
            t0, t1, t2 = [
                turned[part * 24 + t * 8 : part * 24 + t * 8 + 8, x * 128 : x * 128 + 128] for t in range(3)
            ]
            send_ref[pl.ds(row, 4, stride=32), :] = t0[:4]
            send_ref[pl.ds(8 + row, 4, stride=32), :] = t1[:4]
            send_ref[pl.ds(16 + row, 4, stride=32), :] = t2[:4]
            send_ref[pl.ds(24 + row, 4, stride=32), :] = pltpu.roll(t1, 68, axis=1)[:4]


def y_cells(recv_ref, send_ref, stage_ref):
    lane = lanes(4)
    for x in range(NX):
        for part in range(2):
            row = x * 2 + part
            t0, low, t2, high = [recv_ref[pl.ds(slot * 8 + row, 4, stride=32), :] for slot in range(4)]
            at = part * 12
            cut = slice(x * 128, x * 128 + 128)
            stage_ref[at : at + 4, cut] = t0
            stage_ref[at + 4 : at + 8, cut] = jnp.where(lane < 60, low, pltpu.roll(high, 60, axis=1))
            stage_ref[at + 8 : at + 12, cut] = t2
    cells = dot(y_inverse(), stage_ref[...])
    for x in range(NX):
        for row in range(4):
            send_ref[pl.ds(x * 4 + row, GY, stride=16), :] = cells[
                row * 16 : row * 16 + 16, x * 128 : x * 128 + 128
            ]


def x_spectrum(recv_ref, scale):
    found = []
    table = halves(x_forward(scale))
    for tile in range(2):
        data = jnp.concatenate(
            [recv_ref[src * 16 + tile * 8 : src * 16 + tile * 8 + 8, :] for src in range(GX)], axis=0
        )
        found.append(dot(table, data))
    return found


def slots(odd):
    for s in range(6):
        yield 0, s, s + 3 * odd
    for s in range(3):
        yield 1, s, s + 6 * (1 - odd)


def x_cells(mixed, scale, send_ref):
    table = halves(x_inverse(scale))
    for tile in range(2):
        cells = dot(table, mixed[tile])
        for g in range(GX):
            send_ref[g * 16 + tile * 8 : g * 16 + tile * 8 + 8, :] = cells[g * 8 : g * 8 + 8, :]


def weight_row(pair, c):
    return pl.ds(pair * (KX * C) + c, KX, stride=C)


def packed_row(part, c, tile):
    at = ((part * C + c) * 2 + tile) * 16
    return slice(at, at + 16)


def prepare(odd_ref, weight_ref, fields_ref, cotangent_ref, map_ref, packed_ref, direct_ref, cotangent_t_ref, stage_ref):
    pack_weights(odd_ref, weight_ref, packed_ref)
    mapping = halves(map_ref[...])
    stage_ref[...] = jnp.zeros_like(stage_ref)
    for x, y, at in cell_rows():
        stage_ref[at : at + C, :] = dot(mapping, load_cells(fields_ref, x, y), ((0,), (0,)))
    direct_ref[...] = stage_ref[...].T
    for x, y, at in cell_rows():
        stage_ref[at : at + C, :] = load_cells(cotangent_ref, x, y)
    cotangent_t_ref[...] = stage_ref[...].T


def pack_weights(odd_ref, weight_ref, packed_ref):
    odd = odd_ref[0]
    packed_ref[...] = jnp.zeros_like(packed_ref)
    for tile, s, pair in slots(odd):
        for part in range(2):
            for c in range(C):
                at = packed_row(part, c, tile).start
                packed_ref[at : at + KX, 20 * s : 20 * s + C] = weight_ref[weight_row(9 * part + pair, c), :]


def group_start():
    lane = lanes(16)
    return jnp.right_shift(lane * 205, 12) * 20


def pick(a, index):
    return jnp.take_along_axis(a, index, axis=1, mode="promise_in_bounds")


def x_mix(recv_ref, packed_ref, send_ref, spec_ref):
    spectrum = x_spectrum(recv_ref, 1.0)
    start = group_start()
    mixed = []
    for tile in range(2):
        spec_ref[tile * 32 : tile * 32 + 32, :] = spectrum[tile]
        real, imag = spectrum[tile][:16], spectrum[tile][16:]
        out_real = jnp.zeros((16, 128), F32)
        out_imag = jnp.zeros((16, 128), F32)
        for c in range(C):
            index = jnp.minimum(start + c, 127)
            sr, si = pick(real, index), pick(imag, index)
            wr = packed_ref[packed_row(0, c, tile), :]
            wi = packed_ref[packed_row(1, c, tile), :]
            out_real = out_real + (sr * wr - si * wi)
            out_imag = out_imag + (sr * wi + si * wr)
        mixed.append(jnp.concatenate([out_real, out_imag], axis=0))
    x_cells(mixed, INV_CELLS, send_ref)


def x_unmix(recv_ref, spec_ref, packed_ref, share_ref, send_ref, high_ref, low_ref):
    spectrum = x_spectrum(recv_ref, INV_CELLS)
    lane = lanes(KX)
    for part in range(2):
        low, high = part * 16, part * KX
        share_ref[high : high + KX, :] = spec_ref[low : low + KX, :]
        share_ref[24 + high : 24 + high + KX, :] = spectrum[0][low : low + KX]
        dual = pltpu.roll(spectrum[1][low : low + 16], 60, axis=1)[:KX]
        share_ref[48 + high : 48 + high + KX, :] = jnp.where(lane < 60, spec_ref[32 + low : 32 + low + KX, :], dual)
    for tile in range(2):
        dr, di = spectrum[tile][:16], spectrum[tile][16:]
        for c in range(C):
            wr = packed_ref[packed_row(0, c, tile), :]
            wi = packed_ref[packed_row(1, c, tile), :]
            for part, term in enumerate((dr * wr + di * wi, di * wr - dr * wi)):
                high, low = halves(term)
                at = c * 64 + (tile * 2 + part) * 16
                high_ref[at : at + 16, :] = high
                low_ref[at : at + 16, :] = low
    row, col = row_col(128, 128)
    first = jnp.right_shift(row * 205, 12) * 20
    sums = ((col == first) & (row < 120)).astype(F32).astype(jnp.bfloat16)
    found = jnp.dot(high_ref[...], sums, preferred_element_type=F32) + jnp.dot(
        low_ref[...], sums, preferred_element_type=F32
    )
    back = found[:64]
    for c in range(1, C):
        back = back + pltpu.roll(found[c * 64 : c * 64 + 64], c, axis=1)
    x_cells([back[:32], back[32:]], 1.0, send_ref)


def share_parts(share_ref, tile):
    for at in (0, SHARE_ROWS):
        parts = [share_ref[at + k * KX : at + k * KX + KX, :] for k in range(6)]
        if tile == 0:
            yield parts[:4]
        else:
            yield parts[4:] + [pltpu.roll(a, 68, axis=1) for a in parts[4:]]


def add_outer(samples, index, real, imag):
    for er, ei, dr, di in samples:
        sr, si = pick(er, index), pick(ei, index)
        real = real + (sr * dr + si * di)
        imag = imag + (sr * di - si * dr)
    return real, imag


def near_sum(near_ref, sum_ref):
    start = group_start()[:KX]
    zero = jnp.zeros((KX, 128), F32)
    for tile in range(2):
        samples = list(share_parts(near_ref, tile))
        for c in range(C):
            found = add_outer(samples, jnp.minimum(start + c, 127), zero, zero)
            for part in range(2):
                at = packed_row(part, c, tile).start
                sum_ref[at : at + KX, :] = found[part]


def weight_grad(odd_ref, sum_ref, far_ref, grad_hbm, *scratch):
    odd = odd_ref[0]
    buffers, sems = scratch[:2], scratch[2]
    start = group_start()[:KX]
    copies = []
    for tile in range(2):
        buffer, pairs = buffers[tile], (6, 3)[tile]
        samples = list(share_parts(far_ref, tile))
        rows = pairs * KX * C
        for c in range(C):
            near = [sum_ref[packed_row(p, c, tile).start : packed_row(p, c, tile).start + KX, :] for p in range(2)]
            real, imag = add_outer(samples, jnp.minimum(start + c, 127), *near)
            for s in range(pairs):
                buffer[weight_row(s, c), :] = real[:, 20 * s : 20 * s + C]
                buffer[pl.ds(rows + s * (KX * C) + c, KX, stride=C), :] = imag[:, 20 * s : 20 * s + C]
        first = (3 * odd if tile == 0 else 6 * (1 - odd)) * (KX * C)
        for part in range(2):
            copy = pltpu.make_async_copy(
                buffer.at[pl.ds(part * rows, rows), :],
                grad_hbm.at[pl.ds(pl.multiple_of(part * (9 * KX * C) + first, 8), rows), :],
                sems.at[tile * 2 + part],
            )
            copy.start()
            copies.append(copy)
    for copy in copies:
        copy.wait()


def join(mine_ref, other_ref, out_ref):
    out_ref[:SHARE_ROWS, :] = mine_ref[...]
    out_ref[SHARE_ROWS:, :] = other_ref[...]


def emit(map_ref, signal_ref, value_ref, out_ref, direct_ref, stage_ref):
    stage_ref[...] = value_ref[...].T
    for x, y, at in cell_rows():
        store_cells(out_ref, x, y, stage_ref[at : at + C, :])
    stage_ref[...] = signal_ref[...].T
    mapping = halves(map_ref[...])
    for _, _, at in cell_rows():
        direct_ref[at : at + C, :] = dot(mapping, stage_ref[at : at + C, :])
        direct_ref[at + C : at + 32, :] = jnp.zeros((32 - C, NR), F32)


def activate(recv_ref, turned_ref, table_ref, direct_ref, cotangent_ref, value_ref, signal_ref, send_ref, modes_ref):
    high, low = halves(gather_depth(recv_ref, modes_ref))
    both = jnp.concatenate([high, high], axis=0)
    value_ref[...] = (
        jnp.dot(turned_ref[...], both, preferred_element_type=F32)
        + jnp.dot(turned_ref[:, :192], low, preferred_element_type=F32)
        + direct_ref[...]
    )
    k = math.sqrt(2.0 / math.pi)
    for at in range(0, NR, 64):
        cut = slice(at, at + 64)
        v = value_ref[cut, :]
        square = v * v
        th = jnp.tanh(k * (v + 0.044715 * (square * v)))
        half = 0.5 * (1.0 + th)
        value_ref[cut, :] = v * half
        slope = half + 0.5 * v * (1.0 - th * th) * (k * (1.0 + 3 * 0.044715 * square))
        signal_ref[cut, :] = slope * cotangent_ref[cut, :]
    emit_depth(dot(pair(table_ref), signal_ref[...]), send_ref)


def finish(recv_ref, table_ref, direct_ref, out_ref, modes_ref):
    modes = halves(gather_depth(recv_ref, modes_ref))
    spectral = dot(modes, pair(table_ref), ((0,), (0,)))
    for x, y, at in cell_rows():
        store_cells(out_ref, x, y, spectral[at : at + C, :] + direct_ref[at : at + C, :])


def as_rows(a):
    return a.reshape(C * NX, NY, 4, 128).transpose(0, 2, 1, 3).reshape(640, 128)


def from_rows(a):
    return a.reshape(C * NX, 4, NY, 128).transpose(0, 2, 1, 3).reshape(1, C, NX, NY, NR)


CELLS = (256, NR)
TURNED = (NR, 256)
ROWS = (640, 128)
SEND_Y = (GY * 16, 128)
SEND_X = (GX * 16, 128)
PACKED = (2 * C * 2 * 16, 128)
SHARE = (SHARE_ROWS, 128)
BF16 = jnp.bfloat16
DMA = pltpu.SemaphoreType.DMA


def stages():
    base = z_table()
    tz, tz_turned = split_table(base, 0), split_table(base.T.copy(), 1)
    modes = [VMEM((192, 256), F32)]
    return dict(
        depth_forward=lambda f: call(
            depth_forward,
            [SEND_Y],
            *(f, tz),
            scratch=[VMEM(ROWS, F32), VMEM(tz.shape, BF16), VMEM(CELLS, F32), DMA((2,))],
            hbm=(0, 1),
            vmem=66_313_216,
        ),
        prepare=lambda o, w, f, ct, b: call(
            prepare, [PACKED, TURNED, TURNED], o, w, f, ct, b, scratch=[VMEM(CELLS, F32)], smem=(0,)
        ),
        y_spectrum=lambda r: call(y_spectrum, [SEND_X], r),
        y_cells=lambda r: call(y_cells, [SEND_Y], r, scratch=[VMEM((24, 512), F32)]),
        x_mix=lambda r, w: call(x_mix, [SEND_X, (64, 128)], r, w),
        x_unmix=lambda r, s, w: call(x_unmix, [SHARE, SEND_X], *(r, s, w), scratch=[VMEM((64 * C, 128), BF16)] * 2),
        join=lambda a, b: call(join, [(2 * SHARE_ROWS, 128)], a, b),
        emit=lambda b, sig, val: call(emit, [ROWS, CELLS], b, sig, val, scratch=[VMEM(CELLS, F32)]),
        near_sum=lambda near: call(near_sum, [PACKED], near),
        weight_grad=lambda o, near, far: call(
            weight_grad,
            [(2 * 9 * KX * C, C)],
            *(o, near, far),
            scratch=[VMEM((2 * 6 * KX * C, C), F32), VMEM((2 * 3 * KX * C, C), F32), DMA((4,))],
            smem=(0,),
            hbm_out=True,
        ),
        activate=lambda r, d, ct: call(activate, [TURNED, TURNED, SEND_Y], r, tz_turned, tz, d, ct, scratch=modes),
        finish=lambda r, d: call(finish, [ROWS], r, tz, d, scratch=modes),
    )


def swap(a, axis, n):
    rows = a.shape[0] // n
    return lax.all_to_all(
        a.reshape(n, rows, 128), axis, split_axis=0, concat_axis=0, tiled=True
    ).reshape(n * rows, 128)


def on_device(fields, cotangent, spectral, bypass):
    assert lax.axis_size("dp") == 4
    st = stages()
    odd = (lax.axis_index("gx") & 1).astype(jnp.int32).reshape(1)
    rows = as_rows(fields)
    weights = spectral.reshape(2 * 9 * KX * C, C)
    to_y = functools.partial(swap, axis="gy", n=GY)
    to_x = functools.partial(swap, axis="gx", n=GX)
    arrived = to_y(st["depth_forward"](rows))
    packed, direct, turned = st["prepare"](odd, weights, rows, as_rows(cotangent), bypass)
    sent = st["y_spectrum"](arrived)
    mixed, spec = st["x_mix"](to_x(sent), packed)
    arrived = to_y(st["y_cells"](to_x(mixed)))
    value, signal, sent = st["activate"](arrived, direct, turned)
    share, sent = st["x_unmix"](to_x(st["y_spectrum"](to_y(sent))), spec, packed)
    arrived = to_x(sent)
    sent = st["y_cells"](arrived)
    arrived = to_y(sent)
    other = lax.ppermute(share, "dp", [(i, i ^ 1) for i in range(4)])
    joined = st["join"](share, other)
    rest = lax.ppermute(joined, "dp", [(i, 3 - i) for i in range(4)])
    half = st["near_sum"](joined)
    output, direct = st["emit"](bypass, signal, value)
    grad = st["weight_grad"](odd, half, rest)
    field_grad = st["finish"](arrived, direct)
    return (from_rows(output), from_rows(field_grad), grad.reshape(spectral.shape))


def solution(mesh):
    cells = P("dp", None, "gx", "gy", None)
    modes = P(None, "gx", "gy", None, None, None)
    return jax.shard_map(
        on_device,
        mesh=mesh,
        in_specs=(cells, cells, modes, P()),
        out_specs=(cells, cells, modes),
        check_vma=False,
    )
```

```python
import functools
import math

import jax
import jax.numpy as jnp
import numpy as np
from jax import lax
from jax.experimental import pallas as pl
from jax.experimental.pallas import tpu as pltpu
from jax.sharding import PartitionSpec as P


C = 20
NX, NY, NR = 4, 2, 512
GX, GY = 8, 16
S6 = 6
KX = 12
SHARE_ROWS = 6 * KX
F32 = jnp.float32
VMEM = pltpu.VMEM
INV_CELLS = 1.0 / (32 * 32 * 512)
INTERPRET = False


def freq(i, n):
    return i if i < n // 2 else i - n


def z_table():
    r = np.arange(NR)
    z, t = r // 8, r % 8
    out = np.zeros((S6, 2, GY, NR))
    for s in range(S6):
        for j in range(GY):
            m = 6 * j + s
            kz, kt = freq(m // 8, 12), freq(m % 8, 8)
            w = (kz * z * 8 + kt * t * 64) % 512
            ang = w * (2.0 * math.pi / 512)
            out[s, 0, j] = np.cos(ang)
            out[s, 1, j] = -np.sin(ang)
    return out.reshape(S6 * 2 * GY, NR).astype(np.float32)


def split_table(table, axis):
    high = table.astype(jnp.bfloat16)
    low = (table - high.astype(np.float32)).astype(jnp.bfloat16)
    return np.concatenate([high, low], axis=axis)


COS = [(-1) ** i * math.pi ** (2 * i) / math.factorial(2 * i) for i in range(11)]
SIN = [(-1) ** i * math.pi ** (2 * i + 1) / math.factorial(2 * i + 1) for i in range(11)]


def rotation(mode, cell, part_out, part_in, sign, scale):
    k = jnp.where(mode >= 6, mode - 12, mode)
    turns = (((k * cell + 16) & 31) - 16).astype(F32) * (1.0 / 16)
    u = turns * turns
    cos = jnp.full_like(u, COS[-1])
    sin = jnp.full_like(u, SIN[-1])
    for i in range(len(COS) - 2, -1, -1):
        cos = cos * u + COS[i]
        sin = sin * u + SIN[i]
    sin = sin * turns * sign
    value = jnp.where(part_out == part_in, cos, jnp.where(part_out == 1, sin, -sin))
    return value * scale if scale != 1.0 else value


def row_col(rows, cols):
    shape = (rows, cols)
    return lax.broadcasted_iota(jnp.int32, shape, 0), lax.broadcasted_iota(jnp.int32, shape, 1)


def y_forward():
    row, col = row_col(48, 64)
    part = (row >= 24).astype(jnp.int32)
    rest = row - 24 * part
    mode = 3 * (rest & 7) + (rest >> 3)
    return rotation(mode, 2 * (col & 15) + (col >> 5), part, (col >> 4) & 1, -1.0, 1.0)


def y_inverse():
    row, col = row_col(64, 24)
    part = (col >= 12).astype(jnp.int32)
    rest = col - 12 * part
    mode = 3 * (rest & 3) + (rest >> 2)
    return rotation(mode, 2 * (row & 15) + (row >> 5), (row >> 4) & 1, part, 1.0, 1.0)


def x_forward(scale):
    row, col = row_col(32, 64)
    return rotation(row & 15, col >> 1, row >> 4, col & 1, -1.0, scale)


def x_inverse(scale):
    row, col = row_col(64, 32)
    return rotation(col & 15, row >> 1, row & 1, col >> 4, 1.0, scale)


def call(body, outs, *args, scratch=(), smem=(), hbm=(), hbm_out=False, vmem=16 << 20, flops=10**7):
    specs = [
        pl.BlockSpec(memory_space=pltpu.SMEM if i in smem else pltpu.HBM if i in hbm else VMEM)
        for i in range(len(args))
    ]
    shapes = [jax.ShapeDtypeStruct(s, F32) for s in outs]
    nbytes = 4 * sum(math.prod(s) for s in outs) + sum(a.size * a.dtype.itemsize for a in args)
    got = pl.pallas_call(
        body,
        out_shape=shapes,
        in_specs=specs,
        out_specs=[pl.BlockSpec(memory_space=pl.ANY if hbm_out else VMEM)] * len(outs),
        scratch_shapes=list(scratch),
        compiler_params=pltpu.CompilerParams(vmem_limit_bytes=vmem),
        cost_estimate=pl.CostEstimate(flops=flops, bytes_accessed=nbytes, transcendentals=0),
        interpret=INTERPRET,
    )(*args)
    return got if len(outs) > 1 else got[0]


def halves(a):
    high = a.astype(jnp.bfloat16)
    return high, (a - high.astype(F32)).astype(jnp.bfloat16)


def dot(a, b, dims=((1,), (0,))):
    ah, al = a if isinstance(a, tuple) else halves(a)
    bh, bl = b if isinstance(b, tuple) else halves(b)

    def one(x, y):
        return lax.dot_general(x, y, (dims, ((), ())), preferred_element_type=F32)

    return one(ah, bh) + (one(ah, bl) + one(al, bh))


def pair(ref):
    rows = ref.shape[0] // 2
    return ref[:rows, :], ref[rows:, :]


def lanes(rows):
    return lax.broadcasted_iota(jnp.int32, (rows, 128), 1)


def load_cells(ref, x, y):
    return jnp.concatenate(
        [ref[pl.ds(x * 8 + tile * 2 + y, C, stride=32), :] for tile in range(4)], axis=1
    )


def store_cells(ref, x, y, value):
    for tile in range(4):
        ref[pl.ds(x * 8 + tile * 2 + y, C, stride=32), :] = value[:, tile * 128 : tile * 128 + 128]


def emit_depth(modes, send_ref):
    lane = lanes(GY)
    for y in range(NY):
        for x in range(NX):
            for part in range(2):
                total = jnp.zeros((GY, 128), F32)
                for s in range(S6):
                    at = (s * 2 + part) * GY
                    piece = modes[at : at + GY, y * 128 : y * 128 + 128]
                    shift = (20 * s - 32 * x) % 128
                    if shift:
                        piece = pltpu.roll(piece, shift, axis=1)
                    total = jnp.where((lane >= 20 * s) & (lane < 20 * s + 20), piece, total)
                send_ref[pl.ds(x * 4 + y * 2 + part, GY, stride=16), :] = total


def gather_depth(recv_ref, modes_ref):
    lane = lanes(GY)
    for y in range(NY):
        for part in range(2):
            pieces = [recv_ref[pl.ds(x * 4 + y * 2 + part, GY, stride=16), :] for x in range(NX)]
            for s in range(S6):
                total = jnp.zeros((GY, 128), F32)
                for x in range(NX):
                    shift = (32 * x - 20 * s) % 128
                    piece = pltpu.roll(pieces[x], shift, axis=1) if shift else pieces[x]
                    total = jnp.where((lane >= 32 * x) & (lane < 32 * x + 20), piece, total)
                at = (s * 2 + part) * GY
                modes_ref[at : at + GY, y * 128 : y * 128 + 128] = total
    return modes_ref[...]


def cell_rows():
    for y in range(NY):
        for x in range(NX):
            yield x, y, (y * NX + x) * 32


def depth_forward(fields_hbm, table_hbm, send_ref, fields_ref, table_ref, stage_ref, sems):
    fields_copy = pltpu.make_async_copy(fields_hbm, fields_ref, sems.at[0])
    table_copy = pltpu.make_async_copy(table_hbm, table_ref, sems.at[1])
    fields_copy.start()
    table_copy.start()
    stage_ref[...] = jnp.zeros_like(stage_ref)
    fields_copy.wait()
    for x, y, at in cell_rows():
        stage_ref[at : at + C, :] = load_cells(fields_ref, x, y)
    table_copy.wait()
    emit_depth(dot(pair(table_ref), stage_ref[...], ((1,), (1,))), send_ref)


def y_spectrum(recv_ref, send_ref):
    columns = []
    for x in range(NX):
        columns.append(
            jnp.concatenate(
                [recv_ref[pl.ds(x * 4 + row, GY, stride=16), :] for row in range(4)], axis=0
            )
        )
    turned = dot(y_forward(), jnp.concatenate(columns, axis=1))
    for x in range(NX):
        for part in range(2):
            row = x * 2 + part
            t0, t1, t2 = [
                turned[part * 24 + t * 8 : part * 24 + t * 8 + 8, x * 128 : x * 128 + 128] for t in range(3)
            ]
            send_ref[pl.ds(row, 4, stride=32), :] = t0[:4]
            send_ref[pl.ds(8 + row, 4, stride=32), :] = t1[:4]
            send_ref[pl.ds(16 + row, 4, stride=32), :] = t2[:4]
            send_ref[pl.ds(24 + row, 4, stride=32), :] = pltpu.roll(t1, 68, axis=1)[:4]


def y_cells(recv_ref, send_ref, stage_ref):
    lane = lanes(4)
    for x in range(NX):
        for part in range(2):
            row = x * 2 + part
            t0, low, t2, high = [recv_ref[pl.ds(slot * 8 + row, 4, stride=32), :] for slot in range(4)]
            at = part * 12
            cut = slice(x * 128, x * 128 + 128)
            stage_ref[at : at + 4, cut] = t0
            stage_ref[at + 4 : at + 8, cut] = jnp.where(lane < 60, low, pltpu.roll(high, 60, axis=1))
            stage_ref[at + 8 : at + 12, cut] = t2
    cells = dot(y_inverse(), stage_ref[...])
    for x in range(NX):
        for row in range(4):
            send_ref[pl.ds(x * 4 + row, GY, stride=16), :] = cells[
                row * 16 : row * 16 + 16, x * 128 : x * 128 + 128
            ]


def x_spectrum(recv_ref, scale):
    found = []
    table = halves(x_forward(scale))
    for tile in range(2):
        data = jnp.concatenate(
            [recv_ref[src * 16 + tile * 8 : src * 16 + tile * 8 + 8, :] for src in range(GX)], axis=0
        )
        found.append(dot(table, data))
    return found


def slots(odd):
    for s in range(6):
        yield 0, s, s + 3 * odd
    for s in range(3):
        yield 1, s, s + 6 * (1 - odd)


def x_cells(mixed, scale, send_ref):
    table = halves(x_inverse(scale))
    for tile in range(2):
        cells = dot(table, mixed[tile])
        for g in range(GX):
            send_ref[g * 16 + tile * 8 : g * 16 + tile * 8 + 8, :] = cells[g * 8 : g * 8 + 8, :]


def weight_row(pair, c):
    return pl.ds(pair * (KX * C) + c, KX, stride=C)


def packed_row(part, c, tile):
    at = ((part * C + c) * 2 + tile) * 16
    return slice(at, at + 16)


def prepare(odd_ref, weight_ref, fields_ref, cotangent_ref, map_ref, packed_ref, direct_ref, cotangent_t_ref, stage_ref):
    pack_weights(odd_ref, weight_ref, packed_ref)
    mapping = halves(map_ref[...])
    stage_ref[...] = jnp.zeros_like(stage_ref)
    for x, y, at in cell_rows():
        stage_ref[at : at + C, :] = dot(mapping, load_cells(fields_ref, x, y), ((0,), (0,)))
    direct_ref[...] = stage_ref[...].T
    for x, y, at in cell_rows():
        stage_ref[at : at + C, :] = load_cells(cotangent_ref, x, y)
    cotangent_t_ref[...] = stage_ref[...].T


def pack_weights(odd_ref, weight_ref, packed_ref):
    odd = odd_ref[0]
    packed_ref[...] = jnp.zeros_like(packed_ref)
    for tile, s, pair in slots(odd):
        for part in range(2):
            for c in range(C):
                at = packed_row(part, c, tile).start
                packed_ref[at : at + KX, 20 * s : 20 * s + C] = weight_ref[weight_row(9 * part + pair, c), :]


def group_start():
    lane = lanes(16)
    return jnp.right_shift(lane * 205, 12) * 20


def pick(a, index):
    return jnp.take_along_axis(a, index, axis=1, mode="promise_in_bounds")


def x_mix(recv_ref, packed_ref, send_ref, spec_ref):
    spectrum = x_spectrum(recv_ref, 1.0)
    start = group_start()
    mixed = []
    for tile in range(2):
        spec_ref[tile * 32 : tile * 32 + 32, :] = spectrum[tile]
        real, imag = spectrum[tile][:16], spectrum[tile][16:]
        out_real = jnp.zeros((16, 128), F32)
        out_imag = jnp.zeros((16, 128), F32)
        for c in range(C):
            index = jnp.minimum(start + c, 127)
            sr, si = pick(real, index), pick(imag, index)
            wr = packed_ref[packed_row(0, c, tile), :]
            wi = packed_ref[packed_row(1, c, tile), :]
            out_real = out_real + (sr * wr - si * wi)
            out_imag = out_imag + (sr * wi + si * wr)
        mixed.append(jnp.concatenate([out_real, out_imag], axis=0))
    x_cells(mixed, INV_CELLS, send_ref)


def x_unmix(recv_ref, spec_ref, packed_ref, share_ref, send_ref, high_ref, low_ref):
    spectrum = x_spectrum(recv_ref, INV_CELLS)
    lane = lanes(KX)
    for part in range(2):
        low, high = part * 16, part * KX
        share_ref[high : high + KX, :] = spec_ref[low : low + KX, :]
        share_ref[24 + high : 24 + high + KX, :] = spectrum[0][low : low + KX]
        dual = pltpu.roll(spectrum[1][low : low + 16], 60, axis=1)[:KX]
        share_ref[48 + high : 48 + high + KX, :] = jnp.where(lane < 60, spec_ref[32 + low : 32 + low + KX, :], dual)
    for tile in range(2):
        dr, di = spectrum[tile][:16], spectrum[tile][16:]
        for c in range(C):
            wr = packed_ref[packed_row(0, c, tile), :]
            wi = packed_ref[packed_row(1, c, tile), :]
            for part, term in enumerate((dr * wr + di * wi, di * wr - dr * wi)):
                high, low = halves(term)
                at = c * 64 + (tile * 2 + part) * 16
                high_ref[at : at + 16, :] = high
                low_ref[at : at + 16, :] = low
    row, col = row_col(128, 128)
    first = jnp.right_shift(row * 205, 12) * 20
    sums = ((col == first) & (row < 120)).astype(F32).astype(jnp.bfloat16)
    found = jnp.dot(high_ref[...], sums, preferred_element_type=F32) + jnp.dot(
        low_ref[...], sums, preferred_element_type=F32
    )
    back = found[:64]
    for c in range(1, C):
        back = back + pltpu.roll(found[c * 64 : c * 64 + 64], c, axis=1)
    x_cells([back[:32], back[32:]], 1.0, send_ref)


def share_parts(share_ref, tile):
    for at in (0, SHARE_ROWS):
        parts = [share_ref[at + k * KX : at + k * KX + KX, :] for k in range(6)]
        if tile == 0:
            yield parts[:4]
        else:
            yield parts[4:] + [pltpu.roll(a, 68, axis=1) for a in parts[4:]]


def add_outer(samples, index, real, imag):
    for er, ei, dr, di in samples:
        sr, si = pick(er, index), pick(ei, index)
        real = real + (sr * dr + si * di)
        imag = imag + (sr * di - si * dr)
    return real, imag


def near_sum(near_ref, sum_ref):
    start = group_start()[:KX]
    zero = jnp.zeros((KX, 128), F32)
    for tile in range(2):
        samples = list(share_parts(near_ref, tile))
        for c in range(C):
            found = add_outer(samples, jnp.minimum(start + c, 127), zero, zero)
            for part in range(2):
                at = packed_row(part, c, tile).start
                sum_ref[at : at + KX, :] = found[part]


def weight_grad(odd_ref, sum_ref, far_ref, grad_hbm, whole_ref, buffer_ref, sems):
    odd = odd_ref[0]
    start = group_start()[:KX]
    size = KX * C
    copies = []
    for tile in range(2):
        samples = list(share_parts(far_ref, tile))
        for c in range(C):
            at = [packed_row(part, c, tile).start for part in range(2)]
            near = [sum_ref[k : k + KX, :] for k in at]
            found = add_outer(samples, jnp.minimum(start + c, 127), *near)
            for part in range(2):
                whole_ref[at[part] : at[part] + KX, :] = found[part]
        first = 3 * odd if tile == 0 else 6 * (1 - odd)
        for s in range((6, 3)[tile]):
            for part in range(2):
                slot = (tile * 6 + s) * 2 + part
                for c in range(C):
                    k = packed_row(part, c, tile).start
                    buffer_ref[pl.ds(slot * size + c, KX, stride=C), :] = whole_ref[k : k + KX, 20 * s : 20 * s + C]
                copy = pltpu.make_async_copy(
                    buffer_ref.at[pl.ds(slot * size, size), :],
                    grad_hbm.at[pl.ds(pl.multiple_of((9 * part + first + s) * size, 8), size), :],
                    sems.at[slot],
                )
                copy.start()
                copies.append(copy)
    for copy in copies:
        copy.wait()


def join(mine_ref, other_ref, out_ref):
    out_ref[:SHARE_ROWS, :] = mine_ref[...]
    out_ref[SHARE_ROWS:, :] = other_ref[...]


def emit(map_ref, signal_ref, value_ref, out_ref, direct_ref, stage_ref):
    stage_ref[...] = value_ref[...].T
    for x, y, at in cell_rows():
        store_cells(out_ref, x, y, stage_ref[at : at + C, :])
    stage_ref[...] = signal_ref[...].T
    mapping = halves(map_ref[...])
    for _, _, at in cell_rows():
        direct_ref[at : at + C, :] = dot(mapping, stage_ref[at : at + C, :])
        direct_ref[at + C : at + 32, :] = jnp.zeros((32 - C, NR), F32)


def activate(recv_ref, turned_ref, table_ref, direct_ref, cotangent_ref, value_ref, signal_ref, send_ref, modes_ref):
    high, low = halves(gather_depth(recv_ref, modes_ref))
    both = jnp.concatenate([high, high], axis=0)
    value_ref[...] = (
        jnp.dot(turned_ref[...], both, preferred_element_type=F32)
        + jnp.dot(turned_ref[:, :192], low, preferred_element_type=F32)
        + direct_ref[...]
    )
    k = math.sqrt(2.0 / math.pi)
    for at in range(0, NR, 64):
        cut = slice(at, at + 64)
        v = value_ref[cut, :]
        square = v * v
        th = jnp.tanh(k * (v + 0.044715 * (square * v)))
        half = 0.5 * (1.0 + th)
        value_ref[cut, :] = v * half
        slope = half + 0.5 * v * (1.0 - th * th) * (k * (1.0 + 3 * 0.044715 * square))
        signal_ref[cut, :] = slope * cotangent_ref[cut, :]
    emit_depth(dot(pair(table_ref), signal_ref[...]), send_ref)


def finish(recv_ref, table_ref, direct_ref, out_ref, modes_ref):
    modes = halves(gather_depth(recv_ref, modes_ref))
    spectral = dot(modes, pair(table_ref), ((0,), (0,)))
    for x, y, at in cell_rows():
        store_cells(out_ref, x, y, spectral[at : at + C, :] + direct_ref[at : at + C, :])


def as_rows(a):
    return a.reshape(C * NX, NY, 4, 128).transpose(0, 2, 1, 3).reshape(640, 128)


def from_rows(a):
    return a.reshape(C * NX, 4, NY, 128).transpose(0, 2, 1, 3).reshape(1, C, NX, NY, NR)


CELLS = (256, NR)
TURNED = (NR, 256)
ROWS = (640, 128)
SEND_Y = (GY * 16, 128)
SEND_X = (GX * 16, 128)
PACKED = (2 * C * 2 * 16, 128)
SHARE = (SHARE_ROWS, 128)
BF16 = jnp.bfloat16
DMA = pltpu.SemaphoreType.DMA


def stages():
    base = z_table()
    tz, tz_turned = split_table(base, 0), split_table(base.T.copy(), 1)
    modes = [VMEM((192, 256), F32)]
    return dict(
        depth_forward=lambda f: call(
            depth_forward,
            [SEND_Y],
            *(f, tz),
            scratch=[VMEM(ROWS, F32), VMEM(tz.shape, BF16), VMEM(CELLS, F32), DMA((2,))],
            hbm=(0, 1),
            vmem=66_313_216,
        ),
        prepare=lambda o, w, f, ct, b: call(
            prepare, [PACKED, TURNED, TURNED], o, w, f, ct, b, scratch=[VMEM(CELLS, F32)], smem=(0,)
        ),
        y_spectrum=lambda r: call(y_spectrum, [SEND_X], r),
        y_cells=lambda r: call(y_cells, [SEND_Y], r, scratch=[VMEM((24, 512), F32)]),
        x_mix=lambda r, w: call(x_mix, [SEND_X, (64, 128)], r, w),
        x_unmix=lambda r, s, w: call(x_unmix, [SHARE, SEND_X], *(r, s, w), scratch=[VMEM((64 * C, 128), BF16)] * 2),
        join=lambda a, b: call(join, [(2 * SHARE_ROWS, 128)], a, b),
        emit=lambda b, sig, val: call(emit, [ROWS, CELLS], b, sig, val, scratch=[VMEM(CELLS, F32)]),
        near_sum=lambda near: call(near_sum, [PACKED], near),
        weight_grad=lambda o, near, far: call(
            weight_grad,
            [(2 * 9 * KX * C, C)],
            *(o, near, far),
            scratch=[VMEM(PACKED, F32), VMEM((2 * 9 * KX * C, C), F32), DMA((18,))],
            smem=(0,),
            hbm_out=True,
        ),
        activate=lambda r, d, ct: call(activate, [TURNED, TURNED, SEND_Y], r, tz_turned, tz, d, ct, scratch=modes),
        finish=lambda r, d: call(finish, [ROWS], r, tz, d, scratch=modes),
    )


def swap(a, axis, n):
    rows = a.shape[0] // n
    return lax.all_to_all(
        a.reshape(n, rows, 128), axis, split_axis=0, concat_axis=0, tiled=True
    ).reshape(n * rows, 128)


def on_device(fields, cotangent, spectral, bypass):
    assert lax.axis_size("dp") == 4
    st = stages()
    odd = (lax.axis_index("gx") & 1).astype(jnp.int32).reshape(1)
    rows = as_rows(fields)
    weights = spectral.reshape(2 * 9 * KX * C, C)
    to_y = functools.partial(swap, axis="gy", n=GY)
    to_x = functools.partial(swap, axis="gx", n=GX)
    arrived = to_y(st["depth_forward"](rows))
    packed, direct, turned = st["prepare"](odd, weights, rows, as_rows(cotangent), bypass)
    sent = st["y_spectrum"](arrived)
    mixed, spec = st["x_mix"](to_x(sent), packed)
    arrived = to_y(st["y_cells"](to_x(mixed)))
    value, signal, sent = st["activate"](arrived, direct, turned)
    share, sent = st["x_unmix"](to_x(st["y_spectrum"](to_y(sent))), spec, packed)
    arrived = to_x(sent)
    sent = st["y_cells"](arrived)
    arrived = to_y(sent)
    other = lax.ppermute(share, "dp", [(i, 3 - i) for i in range(4)])
    joined = st["join"](share, other)
    rest = lax.ppermute(joined, "dp", [(i, i ^ 1) for i in range(4)])
    half = st["near_sum"](joined)
    output, direct = st["emit"](bypass, signal, value)
    grad = st["weight_grad"](odd, half, rest)
    field_grad = st["finish"](arrived, direct)
    return (from_rows(output), from_rows(field_grad), grad.reshape(spectral.shape))


def solution(mesh):
    cells = P("dp", None, "gx", "gy", None)
    modes = P(None, "gx", "gy", None, None, None)
    return jax.shard_map(
        on_device,
        mesh=mesh,
        in_specs=(cells, cells, modes, P()),
        out_specs=(cells, cells, modes),
        check_vma=False,
    )
```
